32 devices in a mesh: blocks: 32 (over z, y, x, core).
Axes of the slice: x: 2, y: 2, z: 4, core: 2. Of those that a mesh axis runs over, the one named last changes fastest.
Arguments:
- spectra: float32 [1152, 66, 512], P('blocks'), may hold values from 0.05 to 2
- courant: float32 [1152, 3, 512], P('blocks'), may hold values from 0.05 to 0.3
- kernel: bfloat16 [66, 4356], replicated, may hold values from -0.09375 to 0.09375
- old_count: int32 [32], replicated, may hold values from 12 to 36, as said below
- new_count: int32 [32], replicated, may hold values from 12 to 36, as said below
- upwind: int32 [768, 3], replicated, may hold values from 0 to 767, as said below
Outputs:
- updated: float32 [1152, 66, 512], P('blocks')
The draws below stay inside these ranges and needn't reach their ends.
Inputs may be any that keep to these rules, and one draw needn't show every extreme that they name: `old_count`: each count lies in the stated range and both ends are reached in the old and in the new layout; the counts sum to 768; between the two layouts every device boundary along the curve moves by at most 12 blocks, and in every draw some boundary moves by exactly 12 blocks toward higher devices and another by exactly 12 toward lower devices. `new_count`: as old_count, for the new layout. Blocks form aligned runs of 12 along the curve, each run one cross-section of the grid; upwind[b, 0] = b - s * 12 cyclically over 768, where s is +1 or -1 and depends only on b's position within its run, both signs occurring; upwind[b, 1] and upwind[b, 2] lie in the same run as b, arranged alike in every run; every block is upwind of exactly one block per direction.
All inputs are finite; a program needn't handle non-finite values.
Results may differ from the reference program's by a relative error of at most 0.0022.
Values sent between devices are 32-bit elements; how exact they have to be, the bound alone decides.
A program may use at most 128 MiB of HBM per device.

```python
import math
import jax
import jax.numpy as jnp
from jax import lax

BLK_DEV = 24
HALF = 12
CAP = 36
NB = 768
SLOTS = 1152
BINS = 66
EDGE = 8
CELLS = 512
PAIRS = 4356
N_BLOCKS = 32


def boundary_offsets(key):
    base = jax.random.fold_in(key, 4099)
    key_mag, key_sign, key_spot, key_pos = jax.random.split(base, 4)
    device_ids = jnp.arange(N_BLOCKS, dtype=jnp.int32)
    magnitude = jax.random.randint(key_mag, (N_BLOCKS,), HALF // 2, HALF + 1)
    spread_draw = jax.random.randint(key_pos, (N_BLOCKS,), 0, HALF + 1)
    higher = magnitude + spread_draw % (HALF - magnitude + 1)
    lower = higher - magnitude
    upward = jax.random.randint(key_sign, (N_BLOCKS,), 0, 2) == 1
    older = jnp.where(upward, higher, lower)
    newer = jnp.where(upward, lower, higher)
    chosen = jax.random.randint(key_spot, (), 1, N_BLOCKS - 2)
    older = jnp.where(device_ids == 0, 0, older)
    newer = jnp.where(device_ids == 0, 0, newer)
    older = jnp.where(device_ids == chosen - 1, 0, older)
    older = jnp.where(device_ids == chosen, HALF, older)
    older = jnp.where(device_ids == chosen + 1, 0, older)
    newer = jnp.where(device_ids == chosen, 0, newer)
    newer = jnp.where(device_ids == chosen + 1, HALF, newer)
    newer = jnp.where(device_ids == chosen + 2, 0, newer)
    return (older, newer)


def counts_from(offsets):
    return (BLK_DEV + offsets - jnp.roll(offsets, -1)).astype(jnp.int32)


def draw_old_count(key, part):
    return counts_from(boundary_offsets(key)[0])


def draw_new_count(key, part):
    return counts_from(boundary_offsets(key)[1])


def draw_upwind(key, part):
    order = jax.random.permutation(jax.random.fold_in(key, 811), HALF).astype(jnp.int32)
    inverse = jnp.argsort(order).astype(jnp.int32)
    signs = jax.random.randint(jax.random.fold_in(key, 907), (HALF,), 0, 2).astype(jnp.int32) * 2 - 1
    signs = signs.at[order[0]].set(1)
    signs = signs.at[order[1]].set(-1)
    blocks = N_BLOCKS * BLK_DEV
    sections = blocks // HALF
    block_ids = jnp.arange(blocks, dtype=jnp.int32)
    section = block_ids // HALF
    position = block_ids % HALF
    cross = inverse[position]
    across = cross // 2
    depth = cross % 2
    rows_across = HALF // 2
    x_up = (section - signs[position]) % sections * HALF + position
    y_up = section * HALF + order[(across - 1) % rows_across * 2 + depth]
    z_up = section * HALF + order[across * 2 + (1 - depth)]
    return jnp.stack([x_up, y_up, z_up], axis=1).astype(jnp.int32)


def levels(key, dims, cuts, least, high):
    factor_of = 1.0
    for dim, shards_of in cuts:
        draws = jax.random.uniform(jax.random.fold_in(jax.random.fold_in(key, 6), dim), (shards_of,), jnp.float32, least / len(cuts), high / len(cuts))
        factor_of = factor_of * jnp.repeat(jnp.exp(draws), dims[dim] // shards_of).reshape((-1,) + (1,) * (len(dims) - 1 - dim))
    return factor_of


def normal_values(stream_key, extent, scale, most, held_as=jnp.bfloat16):
    entries = scale * jax.random.normal(stream_key, extent, jnp.float32)
    return jnp.clip(entries, min=-most, max=most).astype(held_as)


def setup_inputs(seed: int = 0) -> dict:
    keys = jax.random.split(jax.random.key(seed), 7)
    return {
        "spectra": jnp.clip(jnp.exp(math.log(2.0) - 3.6888794 * jax.random.uniform(keys[0], (SLOTS, BINS, CELLS), jnp.float32) ** levels(keys[0], (SLOTS, BINS, CELLS), ((0, 32),), -0.2, 0.2)), 0.05, 2.0),
        "courant": jnp.clip(0.05 + 0.25 * jax.random.uniform(keys[1], (SLOTS, 3, CELLS), jnp.float32) ** levels(keys[1], (SLOTS, 3, CELLS), ((0, 32),), -0.2, 0.2), 0.05, 0.3),
        "kernel": normal_values(keys[2], (BINS, PAIRS), PAIRS ** -0.5, 0.09375),
        "old_count": draw_old_count(jax.random.fold_in(keys[6], 71), 0),
        "new_count": draw_new_count(jax.random.fold_in(keys[6], 71), 0),
        "upwind": draw_upwind(jax.random.fold_in(keys[6], 71), 0),
    }


def exclusive(counts):
    return jnp.cumsum(counts) - counts


def minmod_value(lower, outer):
    return 0.5 * (jnp.sign(lower) + jnp.sign(outer)) * jnp.minimum(jnp.abs(lower), jnp.abs(outer))


def limited(outer, speeds, upwind_value):
    return speeds * (outer + 0.5 * (1.0 - speeds) * minmod_value(outer - upwind_value, outer))


def slots_of(counts):
    starts = exclusive(counts)
    block_ids = jnp.arange(NB, dtype=jnp.int32)
    owner_ids = jnp.sum((block_ids[:, None] >= starts[None, :]).astype(jnp.int32), axis=1) - 1
    return (owner_ids * CAP + block_ids - starts[owner_ids]).astype(jnp.int32)


def reference(spectra, courant, kernel, old_count, new_count, upwind):
    old_slot = slots_of(old_count)
    state = spectra[old_slot].reshape(NB, BINS, EDGE, EDGE, EDGE)
    speeds = courant[old_slot].reshape(NB, 3, EDGE, EDGE, EDGE)
    fluxes = [speeds[:, direction][:, None] * state for direction in range(3)]
    first = state
    for direction in range(3):
        cell_axis = 2 + direction
        face_in = lax.index_in_dim(fluxes[direction], EDGE - 1, cell_axis, keepdims=True)[upwind[:, direction]]
        inflow = jnp.concatenate([face_in, lax.slice_in_dim(fluxes[direction], 0, EDGE - 1, axis=cell_axis)], axis=cell_axis)
        first = first - fluxes[direction] + inflow
    second = first
    for direction in range(3):
        cell_axis = 2 + direction
        layer_in = lax.index_in_dim(first, EDGE - 1, cell_axis, keepdims=True)[upwind[:, direction]]
        upwind_value = jnp.concatenate([layer_in, lax.slice_in_dim(first, 0, EDGE - 1, axis=cell_axis)], axis=cell_axis)
        cell_flux = limited(first, speeds[:, direction][:, None], upwind_value)
        face_in = lax.index_in_dim(cell_flux, EDGE - 1, cell_axis, keepdims=True)[upwind[:, direction]]
        inflow = jnp.concatenate([face_in, lax.slice_in_dim(cell_flux, 0, EDGE - 1, axis=cell_axis)], axis=cell_axis)
        second = second - cell_flux + inflow
    grouped = second.reshape(NB, BINS, CELLS)

    def coalesce(block):
        pair_terms = (block[:, None, :] * block[None, :, :]).reshape(PAIRS, CELLS).astype(jnp.bfloat16)
        return block + jnp.dot(kernel, pair_terms, preferred_element_type=jnp.float32)

    coalesced = lax.map(coalesce, grouped)
    new_slot = slots_of(new_count)
    return jnp.zeros((SLOTS, BINS, CELLS), jnp.float32).at[new_slot].set(coalesced)
```

```python
import functools

import jax
import jax.numpy as jnp
from jax import lax
from jax.experimental import pallas as pl
from jax.experimental.pallas import tpu as pltpu
from jax.sharding import PartitionSpec as P

HALF = 12
BINS = 66
EDGE = 8
CELLS = 512
TILE = 128
TILES = CELLS // TILE
YZ = 6
XFACES = HALF * 64
PACK = XFACES + 2 * CELLS
EXTRA = 8
ROWS = 72
GROUPS = 288
KDIM = 8 * GROUPS
CHUNK = 4
STRIDES = (64, 8, 1)
ROWSETS = ((0, 32), (32, 64), (64, 66))
VMEM_LIMIT = 63 * 1024 * 1024
F32 = jnp.float32

T_OC, T_NC, T_OS, T_NS = 0, 1, 2, 3
T_SRC = 8
S_COUNT = 0
S_LIST = 8


def position(n, old, new):
    me = lax.axis_index("blocks")

    def total(ref):
        return lax.fori_loop(0, me, lambda i, s: s + ref[i], jnp.int32(0))

    return total(old), total(new), old[me], new[me]


def lane_coord(direction):
    lane = lax.broadcasted_iota(jnp.int32, (1, TILE), 1)
    return (lane // STRIDES[direction]) % EDGE


def low_half():
    return lax.broadcasted_iota(jnp.int32, (1, TILE), 1) < 64


def send_table(capacity, old_start, oc, up, sends):
    zero = jnp.int32(0)
    end_run = lax.rem(old_start + oc, HALF)
    start_run = lax.rem(old_start, HALF)
    for d in (1, 2):

        def link(t, counts):
            s_up, s_dn = counts
            u = up[d, HALF + t] - HALF
            cross = (t >= end_run) & (u < end_run)

            @pl.when(cross)
            def _():
                sends[S_LIST + (d - 1) * 8 + s_up] = jnp.clip(oc - end_run + u, 0, capacity - 1)

            s_up = s_up + cross.astype(jnp.int32)
            cross = (t < start_run) & (u >= start_run)

            @pl.when(cross)
            def _():
                sends[S_LIST + 16 + (d - 1) * 8 + s_dn] = jnp.clip(u - start_run, 0, capacity - 1)

            return s_up, s_dn + cross.astype(jnp.int32)

        s_up, s_dn = lax.fori_loop(0, HALF, link, (zero, zero))
        sends[S_COUNT + d - 1] = jnp.minimum(s_up, YZ)
        sends[S_COUNT + 2 + d - 1] = jnp.minimum(s_dn, YZ)


def plan_kernel(n, capacity, sends, old, new, up, tab):
    old_start, new_start, oc, nc = position(n, old, new)
    tab[T_OC] = oc
    tab[T_NC] = nc
    tab[T_OS] = old_start
    tab[T_NS] = new_start
    tab[T_OC + 4] = sends[S_COUNT]
    end_run = lax.rem(old_start + oc, HALF)
    start_run = lax.rem(old_start, HALF)
    zero = jnp.int32(0)

    def block_src(b, pos):
        at = T_SRC + 8 * b
        u = b + up[0, HALF + pos] - HALF - pos
        above = u >= oc
        remote = above | (u < 0)
        j = jnp.where(above, u - oc, u + HALF)
        base = capacity + jnp.where(above, 4, 0)
        tab[at] = jnp.where(remote, base + (j >> 3), u)
        tab[at + 1] = jnp.where(remote, ((j & 7) >> 1) * TILE, CELLS - TILE)
        tab[at + 2] = jnp.where(remote & ((j & 1) == 0), 64, 0)
        for d in (1, 2):
            tab[at + 1 + 2 * d] = jnp.clip(b + up[d, HALF + pos] - HALF - pos, 0, capacity - 1)
            tab[at + 2 + 2 * d] = TILE - STRIDES[d] * (EDGE - 1)
        return jnp.where(pos == HALF - 1, 0, pos + 1)

    lax.fori_loop(0, capacity, block_src, start_run)

    for d in (1, 2):

        def link(t, counts):
            r_up, r_dn = counts
            u = up[d, HALF + t] - HALF

            def put(b, side, k):
                at = T_SRC + 8 * jnp.clip(b, 0, capacity - 1) + 1 + 2 * d
                tab[at] = capacity + 4 * side + 1 + d
                tab[at + 1] = (TILE - STRIDES[d] * k) & (TILE - 1)

            cross = (t < end_run) & (u >= end_run)

            @pl.when(cross)
            def _():
                put(oc - end_run + t, 1, r_dn)

            r_dn = r_dn + cross.astype(jnp.int32)
            cross = (t >= start_run) & (u < start_run)

            @pl.when(cross)
            def _():
                put(t - start_run, 0, r_up)

            return r_up + cross.astype(jnp.int32), r_dn

        lax.fori_loop(0, HALF, link, (zero, zero))


def pack(oc, sends, field, outs):
    low = low_half()
    coords = [lane_coord(d) for d in range(3)]
    last = pl.ds(CELLS - TILE, TILE)

    def faces(jp, carry):
        for side in range(2):
            first = (oc - HALF if side == 0 else 0) + 2 * jp
            a = field(first, 0, last)
            b = field(first + 1, 0, last)
            for part in range(len(a)):
                lane = pl.multiple_of(part * PACK + jp * TILE, TILE)
                outs[side][:, pl.ds(lane, TILE)] = jnp.where(low, pltpu.roll(a[part], 64, 1), b[part])
        return carry

    lax.fori_loop(0, HALF // 2, faces, 0)
    for side in range(2):
        for d in (1, 2):

            def cross(k, carry, side=side, d=d):
                block = sends[S_LIST + side * 16 + (d - 1) * 8 + k]
                shift = TILE - STRIDES[d] * (EDGE - 1) + STRIDES[d] * k
                for t in range(TILES):
                    values = field(block, d, pl.ds(t * TILE, TILE))
                    for part, value in enumerate(values):
                        lane = part * PACK + XFACES + (d - 1) * CELLS + t * TILE
                        at = pl.ds(lane, TILE)
                        keep = outs[side][:, at]
                        outs[side][:, at] = jnp.where(coords[d] == k, pltpu.roll(value, shift, 1), keep)
                return carry

            lax.fori_loop(0, sends[S_COUNT + side * 2 + d - 1], cross, 0)


def faces_kernel(n, capacity, old, new, upw, q0, speeds, sends, up, dn, cs):
    old_start, _, oc, _ = position(n, old, new)
    send_table(capacity, old_start, oc, upw, sends)
    for b0 in range(0, capacity, 8):
        b1 = min(b0 + 8, capacity)
        for t in range(TILES):
            at = pl.ds(t * TILE, TILE)
            cs[b0:b1, :, at] = jnp.swapaxes(speeds[:, b0:b1, at], 0, 1)

    def field(block, d, lanes):
        return (q0[block, :, lanes] * cs[block, d : d + 1, lanes],)

    pack(oc, sends, field, (up, dn))


def spread(capacity, packets, part, targets, sems):
    copies = []
    for side, packet in enumerate(packets):
        base = part * PACK
        slot = capacity + 4 * side
        pieces = (
            (0, 0, CELLS),
            (1, CELLS, XFACES - CELLS),
            (2, XFACES, CELLS),
            (3, XFACES + CELLS, CELLS),
        )
        for i, (sub, lane, width) in enumerate(pieces):
            target = targets[max(sub - 1, 0)]
            copies.append(
                pltpu.make_async_copy(
                    packet.at[:, pl.ds(base + lane, width)],
                    target.at[slot + sub, :, pl.ds(0, width)],
                    sems.at[4 * side + i],
                )
            )
    return copies


def sources(tab, b):
    at = T_SRC + 8 * b
    sx, tx, rx, sy, ry, sz, rz = [tab[at + i] for i in range(7)]
    return sx, pl.ds(pl.multiple_of(tx, TILE), TILE), rx, sy, ry, sz, rz


def first_kernel(capacity, tab, sends, q0, cs, from_prev, from_next, q1, up, dn, qx, cx, sem, sems):
    load = pltpu.make_async_copy(q0, qx.at[pl.ds(0, capacity)], sem)
    load.start()
    copies = spread(capacity, (from_prev, from_next), 0, (qx, qx, qx), sems)
    for copy in copies:
        copy.start()
    table = pltpu.make_async_copy(cs, cx.at[pl.ds(0, capacity)], sems.at[8])
    table.start()
    copies.append(table)
    for i in range(EXTRA):
        cx[capacity + i] = jnp.ones((3, CELLS), F32)
    for copy in copies:
        copy.wait()
    load.wait()
    low = low_half()
    y0, z0 = lane_coord(1) == 0, lane_coord(2) == 0
    oc = tab[T_OC]

    def step(b, carry):
        sx, tx, rx, sy, ry, sz, rz = sources(tab, b)
        before = None
        for t in range(TILES):
            at = pl.ds(t * TILE, TILE)
            c = [cx[b, d : d + 1, at] for d in range(3)]
            keep = 1.0 - c[0] - c[1] - c[2]
            cuy, cuz = cx[sy, 1:2, at], cx[sz, 2:3, at]
            if t == 0:
                cux = cx[sx, 0:1, tx]
            else:
                cm = jnp.where(low, c[0], before)
            for r0, r1 in ROWSETS:
                q = qx[b, r0:r1, at]
                if t == 0:
                    far = pltpu.roll(qx[sx, r0:r1, tx] * cux, rx, 1)
                    mixed = jnp.where(low, q * c[0], far)
                else:
                    mixed = jnp.where(low, q, qx[b, r0:r1, pl.ds((t - 1) * TILE, TILE)]) * cm
                inx = pltpu.roll(mixed, 64, 1)
                iny = jnp.where(
                    y0, pltpu.roll(qx[sy, r0:r1, at] * cuy, ry, 1), pltpu.roll(q * c[1], 8, 1)
                )
                inz = jnp.where(
                    z0, pltpu.roll(qx[sz, r0:r1, at] * cuz, rz, 1), pltpu.roll(q * c[2], 1, 1)
                )
                q1[b, r0:r1, at] = q * keep + (inx + (iny + inz))
            before = c[0]
        return carry

    lax.fori_loop(0, oc, step, 0)

    def field(block, d, lanes):
        q = q1[block, :, lanes]
        c = cx[block, d : d + 1, lanes]
        m = q - pltpu.roll(q, STRIDES[d], 1)
        m = jnp.maximum(jnp.minimum(m, q), 0.0)
        return c * q + (0.5 * c * (1.0 - c)) * m, q

    pack(oc, sends, field, (up, dn))


def second_kernel(
    capacity, tab, q1, cs, from_prev, from_next, q2out, *rest
):
    chunks = HALF // CHUNK
    ups, dns = rest[:chunks], rest[chunks : 2 * chunks]
    qx, fx, fy, fz, q2, sem, lsems, fsems, osems = rest[2 * chunks :]
    fluxes = (fx, fy, fz)
    packets = (from_prev, from_next)
    load = pltpu.make_async_copy(q1, qx.at[pl.ds(0, capacity)], sem)
    load.start()
    copies = spread(capacity, packets, 1, (qx, qx, qx), lsems)
    copies += spread(capacity, packets, 0, fluxes, fsems)
    for copy in copies:
        copy.start()
    for copy in copies:
        copy.wait()
    load.wait()
    low = low_half()
    y0, z0 = lane_coord(1) == 0, lane_coord(2) == 0
    oc = tab[T_OC]

    def limit(b, carry):
        sx, tx, rx, sy, ry, sz, rz = sources(tab, b)
        for t in range(TILES):
            at = pl.ds(t * TILE, TILE)
            c = [cs[b, d : d + 1, at] for d in range(3)]
            half = [0.5 * v * (1.0 - v) for v in c]
            for r0, r1 in ROWSETS:
                q = qx[b, r0:r1, at]
                if t == 0:
                    far = pltpu.roll(qx[sx, r0:r1, tx], rx, 1)
                else:
                    far = qx[b, r0:r1, pl.ds((t - 1) * TILE, TILE)]
                before = (
                    pltpu.roll(jnp.where(low, q, far), 64, 1),
                    jnp.where(y0, pltpu.roll(qx[sy, r0:r1, at], ry, 1), pltpu.roll(q, 8, 1)),
                    jnp.where(z0, pltpu.roll(qx[sz, r0:r1, at], rz, 1), pltpu.roll(q, 1, 1)),
                )
                rest = q
                for d in range(3):
                    m = jnp.maximum(jnp.minimum(q - before[d], q), 0.0)
                    flux = c[d] * q + half[d] * m
                    fluxes[d][b, r0:r1, at] = flux
                    rest = rest - flux
                q2[b, r0:r1, at] = rest
        return carry

    lax.fori_loop(0, oc, limit, 0)

    def step(b, carry):
        sx, tx, rx, sy, ry, sz, rz = sources(tab, b)
        for t in range(TILES):
            at = pl.ds(t * TILE, TILE)
            for r0, r1 in ROWSETS:
                if t == 0:
                    far = pltpu.roll(fx[sx, r0:r1, tx], rx, 1)
                else:
                    far = fx[b, r0:r1, pl.ds((t - 1) * TILE, TILE)]
                inx = pltpu.roll(jnp.where(low, fx[b, r0:r1, at], far), 64, 1)
                iny = jnp.where(
                    y0, pltpu.roll(fy[sy, r0:r1, at], ry, 1), pltpu.roll(fy[b, r0:r1, at], 8, 1)
                )
                inz = jnp.where(
                    z0, pltpu.roll(fz[sz, r0:r1, at], rz, 1), pltpu.roll(fz[b, r0:r1, at], 1, 1)
                )
                q2[b, r0:r1, at] = q2[b, r0:r1, at] + (inx + (iny + inz))
        return carry

    lax.fori_loop(0, oc, step, 0)
    outs = [pltpu.make_async_copy(q2, q2out, osems.at[0])]
    for c in range(chunks):
        outs.append(
            pltpu.make_async_copy(
                q2.at[pl.ds(oc - HALF + c * CHUNK, CHUNK)], ups[c], osems.at[1 + c]
            )
        )
        outs.append(
            pltpu.make_async_copy(
                q2.at[pl.ds(c * CHUNK, CHUNK)], dns[c], osems.at[1 + chunks + c]
            )
        )
    for copy in outs:
        copy.start()
    for copy in outs:
        copy.wait()


def build_pairs(q, qp, pairs):
    qp[0:BINS, :] = q
    qp[BINS:ROWS, :] = jnp.zeros((ROWS - BINS, CELLS), F32)
    pending = []

    def emit(term):
        pending.append(term)
        if len(pending) % 2 == 0:
            at = 8 * (len(pending) - 2)
            tile = jnp.concatenate(pending[-2:], axis=0)
            pairs[at : at + 16, :] = tile.astype(jnp.bfloat16)

    def lead(i):
        return jnp.broadcast_to(qp[i : i + 1, :], (8, CELLS))

    def group(g):
        return qp[8 * g : 8 * g + 8, :]

    for a in range(7):
        for r in range(8):
            by = lead(8 * a + r)
            for b in range(a + 1, 8):
                emit(by * group(b))
    for e in (BINS - 2, BINS - 1):
        by = lead(e)
        for a in range(8):
            emit(by * group(a))
    for a in range(8):
        g = group(a)
        emit(g * g)
        for k in range(1, 5):
            emit(g * pltpu.roll(g, 8 - k, 0))
    tail = group(8)
    emit(tail * tail)
    emit(lead(BINS - 1) * tail)
    while len(pending) < GROUPS:
        emit(jnp.zeros((8, CELLS), F32))


def coalesce(count, load, slot_of, w, out, qps, pairs, res, sems):
    def copy_out(slot, buf):
        return pltpu.make_async_copy(res.at[buf], out.at[slot], sems.at[buf])

    def body(it, carry):
        first = 2 * it
        items = (first, jnp.minimum(first + 1, count - 1))
        values = [load(i) for i in items]

        @pl.when(it > 0)
        def _():
            for buf in range(2):
                copy_out(0, buf).wait()

        for buf in range(2):
            build_pairs(values[buf], qps[buf], pairs[buf])
        for buf in range(2):
            gain = jnp.dot(w[...], pairs[buf][...], preferred_element_type=F32)
            res[buf] = qps[buf][0:BINS, :] + gain
        copy_out(slot_of(items[0]), 0).start()

        @pl.when(first + 1 < count)
        def _():
            copy_out(slot_of(items[1]), 1).start()

        return carry

    trips = lax.div(count + 1, 2)
    lax.fori_loop(0, trips, body, 0)

    @pl.when(trips > 0)
    def _():
        copy_out(0, 0).wait()

    @pl.when((trips > 0) & (lax.rem(count, 2) == 0))
    def _():
        copy_out(0, 1).wait()


def ranges(tab):
    oc, nc, old, new = tab[T_OC], tab[T_NC], tab[T_OS], tab[T_NS]
    lo = jnp.clip(old - new, 0, nc)
    hi = jnp.clip(old + oc - new, lo, nc)
    return lo, hi, nc, new - old


def stay_kernel(capacity, tab, q2, w, out, qpa, qpb, pa, pb, res, zero, sems, zsem):
    lo, hi, nc, shift = ranges(tab)
    zero[...] = jnp.zeros_like(zero)

    def blank(slot):
        return pltpu.make_async_copy(zero, out.at[slot], zsem)

    def start(slot, carry):
        blank(slot).start()
        return carry

    def wait(slot, carry):
        blank(slot).wait()
        return carry

    lax.fori_loop(nc, capacity, start, 0)
    coalesce(
        hi - lo,
        lambda i: q2[i + lo + shift],
        lambda i: i + lo,
        w,
        out,
        (qpa, qpb),
        (pa, pb),
        res,
        sems,
    )
    lax.fori_loop(nc, capacity, wait, 0)


def come_kernel(c, tab, from_prev, from_next, w, old_out, out, qpa, qpb, pa, pb, res, src, sems, lsems):
    lo, hi, nc, _ = ranges(tab)
    loads = [
        pltpu.make_async_copy(ref, src.at[pl.ds(side * CHUNK, CHUNK)], lsems.at[side])
        for side, ref in enumerate((from_prev, from_next))
    ]
    for copy in loads:
        copy.start()
    for copy in loads:
        copy.wait()
    skip = jnp.clip(HALF - lo - c * CHUNK, 0, CHUNK)
    ups = CHUNK - skip
    downs = jnp.clip(nc - hi - c * CHUNK, 0, CHUNK)
    slot_up = c * CHUNK + skip - HALF + lo
    slot_dn = hi + c * CHUNK
    coalesce(
        ups + downs,
        lambda i: src[jnp.where(i < ups, i + skip, i - ups + CHUNK)],
        lambda i: jnp.where(i < ups, i + slot_up, i - ups + slot_dn),
        w,
        out,
        (qpa, qpb),
        (pa, pb),
        res,
        sems,
    )


def folded_kernel(kernel):
    cube = kernel.reshape(BINS, BINS, BINS).astype(F32)
    both = cube + jnp.swapaxes(cube, 1, 2)
    a, b = BINS - 2, BINS - 1
    parts = [both[:, 8 * g : 8 * g + 8, 8 * g + 8 : a].reshape(BINS, -1) for g in range(7)]
    parts += [both[:, a, :a], both[:, b, :a]]
    s = lax.broadcasted_iota(jnp.int32, (1, 8, 8), 1)
    t = lax.broadcasted_iota(jnp.int32, (1, 8, 8), 2)
    for g in range(8):
        at = slice(8 * g, 8 * g + 8)
        for k in range(5):
            block = (both if 0 < k < 4 else cube)[:, at, at]
            parts.append(jnp.sum(jnp.where(t == (s + k) % 8, block, 0.0), axis=2))
    zero = jnp.zeros((BINS, 6), F32)
    parts += [cube[:, a, a][:, None], cube[:, b, b][:, None], zero]
    parts += [both[:, a, b][:, None], jnp.zeros((BINS, 7), F32)]
    width = sum(p.shape[1] for p in parts)
    parts.append(jnp.zeros((BINS, KDIM - width), F32))
    return jnp.concatenate([p.astype(jnp.bfloat16) for p in parts], axis=1)


def on_device(n, spectra, courant, kernel, old_count, new_count, upwind):
    capacity = spectra.shape[0]
    shape = jax.ShapeDtypeStruct
    vmem = pl.BlockSpec(memory_space=pltpu.VMEM)
    smem = pl.BlockSpec(memory_space=pltpu.SMEM)
    hbm = pl.BlockSpec(memory_space=pl.ANY)
    params = pltpu.CompilerParams(vmem_limit_bytes=VMEM_LIMIT)
    blocks = shape((capacity, BINS, CELLS), F32)
    chunk = shape((CHUNK, BINS, CELLS), F32)
    chunks = HALF // CHUNK
    wide = pltpu.VMEM((capacity + EXTRA, BINS, CELLS), F32)
    dma = pltpu.SemaphoreType.DMA

    def cost(flops, nbytes):
        return pl.CostEstimate(flops=flops, bytes_accessed=nbytes, transcendentals=0)

    upw = jnp.swapaxes(upwind, 0, 1)
    sends, up, dn, cs = pl.pallas_call(
        functools.partial(faces_kernel, n, capacity),
        out_shape=(
            shape((S_LIST + 32,), jnp.int32),
            shape((BINS, PACK), F32),
            shape((BINS, PACK), F32),
            shape((capacity, 3, CELLS), F32),
        ),
        in_specs=[smem, smem, smem, vmem, vmem],
        out_specs=(smem, vmem, vmem, vmem),
        compiler_params=params,
        name="faces",
    )(old_count, new_count, upw, spectra, jnp.swapaxes(courant, 0, 1))

    def along(value, step, ring):
        route = [(i, i + step) for i in range(n)]
        if ring:
            route = [(i, j % n) for i, j in route]
        return lax.ppermute(value, "blocks", [(i, j) for i, j in route if 0 <= j < n])

    from_prev, from_next = along(up, 1, True), along(dn, -1, True)
    tab = pl.pallas_call(
        functools.partial(plan_kernel, n, capacity),
        out_shape=shape((T_SRC + 8 * capacity,), jnp.int32),
        in_specs=[smem] * 4,
        out_specs=smem,
        cost_estimate=cost(1000000, 1000000),
        name="plan",
    )(sends, old_count, new_count, upw)
    weights = folded_kernel(kernel)
    packed = shape((BINS, 2 * PACK), F32)
    q1, up, dn = pl.pallas_call(
        functools.partial(first_kernel, capacity),
        out_shape=(blocks, packed, packed),
        in_specs=[smem, smem, hbm, hbm, hbm, hbm],
        out_specs=(vmem, vmem, vmem),
        scratch_shapes=[
            wide,
            pltpu.VMEM((capacity + EXTRA, 3, CELLS), F32),
            dma,
            dma((9,)),
        ],
        compiler_params=params,
        name="first",
    )(tab, sends, spectra, cs, from_prev, from_next)
    from_prev, from_next = along(up, 1, True), along(dn, -1, True)
    q1, weights = lax.optimization_barrier((q1, weights))
    q2, *moved = pl.pallas_call(
        functools.partial(second_kernel, capacity),
        out_shape=[blocks] + [chunk] * (2 * chunks),
        in_specs=[smem, hbm, vmem, hbm, hbm],
        out_specs=[hbm] * (1 + 2 * chunks),
        scratch_shapes=[
            wide,
            wide,
            wide,
            wide,
            pltpu.VMEM((capacity, BINS, CELLS), F32),
            dma,
            dma((8,)),
            dma((8,)),
            dma((1 + 2 * chunks,)),
        ],
        compiler_params=params,
        name="second",
    )(tab, q1, cs, from_prev, from_next)
    arrived = [
        (along(moved[c], 1, False), along(moved[chunks + c], -1, False)) for c in range(chunks)
    ]
    buffers = [
        pltpu.VMEM((ROWS, CELLS), F32),
        pltpu.VMEM((ROWS, CELLS), F32),
        pltpu.VMEM((KDIM, CELLS), jnp.bfloat16),
        pltpu.VMEM((KDIM, CELLS), jnp.bfloat16),
        pltpu.VMEM((2, BINS, CELLS), F32),
    ]
    work = 2 * BINS * KDIM * CELLS
    updated = pl.pallas_call(
        functools.partial(stay_kernel, capacity),
        out_shape=blocks,
        in_specs=[smem, vmem, vmem],
        out_specs=hbm,
        scratch_shapes=buffers + [pltpu.VMEM((BINS, CELLS), F32), dma((2,)), dma],
        compiler_params=params,
        cost_estimate=cost(24 * work, 12 * 1024 * 1024),
        name="stay",
    )(tab, q2, weights)
    for c in range(chunks):
        updated = pl.pallas_call(
            functools.partial(come_kernel, c),
            out_shape=blocks,
            in_specs=[smem, hbm, hbm, vmem, hbm],
            out_specs=hbm,
            input_output_aliases={4: 0},
            scratch_shapes=buffers
            + [pltpu.VMEM((2 * CHUNK, BINS, CELLS), F32), dma((2,)), dma((2,))],
            compiler_params=params,
            cost_estimate=cost(8 * work, 4 * 1024 * 1024),
            name=f"come{c}",
        )(tab, *arrived[c], weights, updated)
    return updated


def solution(mesh):
    in_specs = (P("blocks", None, None), P("blocks", None, None), P(), P(), P(), P())
    out_specs = P("blocks", None, None)
    return jax.shard_map(
        functools.partial(on_device, mesh.shape["blocks"]),
        mesh=mesh,
        in_specs=in_specs,
        out_specs=out_specs,
        check_vma=False,
    )
```

```python
import functools

import jax
import jax.numpy as jnp
from jax import lax
from jax.experimental import pallas as pl
from jax.experimental.pallas import tpu as pltpu
from jax.sharding import PartitionSpec as P

HALF = 12
BINS = 66
EDGE = 8
CELLS = 512
TILE = 128
TILES = CELLS // TILE
YZ = 6
XFACES = HALF * 64
PACK = XFACES + 2 * CELLS
EXTRA = 8
ROWS = 72
GROUPS = 288
KDIM = 8 * GROUPS
CHUNK = 4
MAIN = 64
STRIDES = (64, 8, 1)
ROWSETS = ((0, 32), (32, 64), (64, 66))
VMEM_LIMIT = 63 * 1024 * 1024
F32 = jnp.float32

T_OC, T_NC, T_OS, T_NS = 0, 1, 2, 3
T_SRC = 8
S_COUNT = 0
S_LIST = 8


def position(n, old, new):
    me = lax.axis_index("blocks")

    def total(ref):
        return lax.fori_loop(0, me, lambda i, s: s + ref[i], jnp.int32(0))

    return total(old), total(new), old[me], new[me]


def lane_coord(direction):
    lane = lax.broadcasted_iota(jnp.int32, (1, TILE), 1)
    return (lane // STRIDES[direction]) % EDGE


def low_half():
    return lax.broadcasted_iota(jnp.int32, (1, TILE), 1) < 64


def send_table(capacity, old_start, oc, up, sends):
    zero = jnp.int32(0)
    end_run = lax.rem(old_start + oc, HALF)
    start_run = lax.rem(old_start, HALF)
    for d in (1, 2):

        def link(t, counts):
            s_up, s_dn = counts
            u = up[d, HALF + t] - HALF
            cross = (t >= end_run) & (u < end_run)

            @pl.when(cross)
            def _():
                sends[S_LIST + (d - 1) * 8 + s_up] = jnp.clip(oc - end_run + u, 0, capacity - 1)

            s_up = s_up + cross.astype(jnp.int32)
            cross = (t < start_run) & (u >= start_run)

            @pl.when(cross)
            def _():
                sends[S_LIST + 16 + (d - 1) * 8 + s_dn] = jnp.clip(u - start_run, 0, capacity - 1)

            return s_up, s_dn + cross.astype(jnp.int32)

        s_up, s_dn = lax.fori_loop(0, HALF, link, (zero, zero))
        sends[S_COUNT + d - 1] = jnp.minimum(s_up, YZ)
        sends[S_COUNT + 2 + d - 1] = jnp.minimum(s_dn, YZ)


def plan_kernel(n, capacity, sends, old, new, up, tab):
    old_start, new_start, oc, nc = position(n, old, new)
    tab[T_OC] = oc
    tab[T_NC] = nc
    tab[T_OS] = old_start
    tab[T_NS] = new_start
    tab[T_OC + 4] = sends[S_COUNT]
    end_run = lax.rem(old_start + oc, HALF)
    start_run = lax.rem(old_start, HALF)
    zero = jnp.int32(0)

    def block_src(b, pos):
        at = T_SRC + 8 * b
        u = b + up[0, HALF + pos] - HALF - pos
        above = u >= oc
        remote = above | (u < 0)
        j = jnp.where(above, u - oc, u + HALF)
        base = capacity + jnp.where(above, 4, 0)
        tab[at] = jnp.where(remote, base + (j >> 3), u)
        tab[at + 1] = jnp.where(remote, ((j & 7) >> 1) * TILE, CELLS - TILE)
        tab[at + 2] = jnp.where(remote & ((j & 1) == 0), 64, 0)
        for d in (1, 2):
            tab[at + 1 + 2 * d] = jnp.clip(b + up[d, HALF + pos] - HALF - pos, 0, capacity - 1)
            tab[at + 2 + 2 * d] = TILE - STRIDES[d] * (EDGE - 1)
        return jnp.where(pos == HALF - 1, 0, pos + 1)

    lax.fori_loop(0, capacity, block_src, start_run)

    for d in (1, 2):

        def link(t, counts):
            r_up, r_dn = counts
            u = up[d, HALF + t] - HALF

            def put(b, side, k):
                at = T_SRC + 8 * jnp.clip(b, 0, capacity - 1) + 1 + 2 * d
                tab[at] = capacity + 4 * side + 1 + d
                tab[at + 1] = (TILE - STRIDES[d] * k) & (TILE - 1)

            cross = (t < end_run) & (u >= end_run)

            @pl.when(cross)
            def _():
                put(oc - end_run + t, 1, r_dn)

            r_dn = r_dn + cross.astype(jnp.int32)
            cross = (t >= start_run) & (u < start_run)

            @pl.when(cross)
            def _():
                put(t - start_run, 0, r_up)

            return r_up + cross.astype(jnp.int32), r_dn

        lax.fori_loop(0, HALF, link, (zero, zero))


def pack(oc, sends, field, outs):
    low = low_half()
    coords = [lane_coord(d) for d in range(3)]
    last = pl.ds(CELLS - TILE, TILE)

    def faces(jp, carry):
        for side in range(2):
            first = (oc - HALF if side == 0 else 0) + 2 * jp
            a = field(first, 0, last)
            b = field(first + 1, 0, last)
            for part in range(len(a)):
                lane = pl.multiple_of(part * PACK + jp * TILE, TILE)
                outs[side][:, pl.ds(lane, TILE)] = jnp.where(low, pltpu.roll(a[part], 64, 1), b[part])
        return carry

    lax.fori_loop(0, HALF // 2, faces, 0)
    for side in range(2):
        for d in (1, 2):

            def cross(k, carry, side=side, d=d):
                block = sends[S_LIST + side * 16 + (d - 1) * 8 + k]
                shift = TILE - STRIDES[d] * (EDGE - 1) + STRIDES[d] * k
                for t in range(TILES):
                    values = field(block, d, pl.ds(t * TILE, TILE))
                    for part, value in enumerate(values):
                        lane = part * PACK + XFACES + (d - 1) * CELLS + t * TILE
                        at = pl.ds(lane, TILE)
                        keep = outs[side][:, at]
                        outs[side][:, at] = jnp.where(coords[d] == k, pltpu.roll(value, shift, 1), keep)
                return carry

            lax.fori_loop(0, sends[S_COUNT + side * 2 + d - 1], cross, 0)


def faces_kernel(n, capacity, old, new, upw, q0, speeds, sends, up, dn, cs):
    old_start, _, oc, _ = position(n, old, new)
    send_table(capacity, old_start, oc, upw, sends)
    for b0 in range(0, capacity, 8):
        b1 = min(b0 + 8, capacity)
        for t in range(TILES):
            at = pl.ds(t * TILE, TILE)
            cs[b0:b1, :, at] = jnp.swapaxes(speeds[:, b0:b1, at], 0, 1)

    def field(block, d, lanes):
        return (q0[block, :, lanes] * cs[block, d : d + 1, lanes],)

    pack(oc, sends, field, (up, dn))


def spread(capacity, packets, part, targets, sems):
    copies = []
    for side, packet in enumerate(packets):
        base = part * PACK
        slot = capacity + 4 * side
        pieces = (
            (0, 0, CELLS),
            (1, CELLS, XFACES - CELLS),
            (2, XFACES, CELLS),
            (3, XFACES + CELLS, CELLS),
        )
        for i, (sub, lane, width) in enumerate(pieces):
            target = targets[max(sub - 1, 0)]
            copies.append(
                pltpu.make_async_copy(
                    packet.at[:, pl.ds(base + lane, width)],
                    target.at[slot + sub, :, pl.ds(0, width)],
                    sems.at[4 * side + i],
                )
            )
    return copies


def sources(tab, b):
    at = T_SRC + 8 * b
    sx, tx, rx, sy, ry, sz, rz = [tab[at + i] for i in range(7)]
    return sx, pl.ds(pl.multiple_of(tx, TILE), TILE), rx, sy, ry, sz, rz


def first_kernel(capacity, tab, sends, q0, cs, from_prev, from_next, q1, up, dn, qx, cx, sem, sems):
    load = pltpu.make_async_copy(q0, qx.at[pl.ds(0, capacity)], sem)
    load.start()
    copies = spread(capacity, (from_prev, from_next), 0, (qx, qx, qx), sems)
    for copy in copies:
        copy.start()
    table = pltpu.make_async_copy(cs, cx.at[pl.ds(0, capacity)], sems.at[8])
    table.start()
    copies.append(table)
    for i in range(EXTRA):
        cx[capacity + i] = jnp.ones((3, CELLS), F32)
    for copy in copies:
        copy.wait()
    load.wait()
    low = low_half()
    y0, z0 = lane_coord(1) == 0, lane_coord(2) == 0
    oc = tab[T_OC]

    def step(b, carry):
        sx, tx, rx, sy, ry, sz, rz = sources(tab, b)
        before = None
        for t in range(TILES):
            at = pl.ds(t * TILE, TILE)
            c = [cx[b, d : d + 1, at] for d in range(3)]
            keep = 1.0 - c[0] - c[1] - c[2]
            cuy, cuz = cx[sy, 1:2, at], cx[sz, 2:3, at]
            if t == 0:
                cux = cx[sx, 0:1, tx]
            else:
                cm = jnp.where(low, c[0], before)
            for r0, r1 in ROWSETS:
                q = qx[b, r0:r1, at]
                if t == 0:
                    far = pltpu.roll(qx[sx, r0:r1, tx] * cux, rx, 1)
                    mixed = jnp.where(low, q * c[0], far)
                else:
                    mixed = jnp.where(low, q, qx[b, r0:r1, pl.ds((t - 1) * TILE, TILE)]) * cm
                inx = pltpu.roll(mixed, 64, 1)
                iny = jnp.where(
                    y0, pltpu.roll(qx[sy, r0:r1, at] * cuy, ry, 1), pltpu.roll(q * c[1], 8, 1)
                )
                inz = jnp.where(
                    z0, pltpu.roll(qx[sz, r0:r1, at] * cuz, rz, 1), pltpu.roll(q * c[2], 1, 1)
                )
                q1[b, r0:r1, at] = q * keep + (inx + (iny + inz))
            before = c[0]
        return carry

    lax.fori_loop(0, oc, step, 0)

    def field(block, d, lanes):
        q = q1[block, :, lanes]
        c = cx[block, d : d + 1, lanes]
        m = q - pltpu.roll(q, STRIDES[d], 1)
        m = jnp.maximum(jnp.minimum(m, q), 0.0)
        return c * q + (0.5 * c * (1.0 - c)) * m, q

    pack(oc, sends, field, (up, dn))


def second_kernel(
    capacity, tab, q1, cs, from_prev, from_next, q2out, *rest
):
    chunks = HALF // CHUNK
    ups, dns = rest[:chunks], rest[chunks : 2 * chunks]
    qx, fx, fy, fz, q2, tails, sem, lsems, fsems, osems, msems = rest[2 * chunks :]
    fluxes = (fx, fy, fz)
    packets = (from_prev, from_next)
    load = pltpu.make_async_copy(q1, qx.at[pl.ds(0, capacity)], sem)
    load.start()
    copies = spread(capacity, packets, 1, (qx, qx, qx), lsems)
    copies += spread(capacity, packets, 0, fluxes, fsems)
    for copy in copies:
        copy.start()
    for copy in copies:
        copy.wait()
    load.wait()
    low = low_half()
    y0, z0 = lane_coord(1) == 0, lane_coord(2) == 0
    oc = tab[T_OC]

    def limit(b, carry):
        sx, tx, rx, sy, ry, sz, rz = sources(tab, b)
        for t in range(TILES):
            at = pl.ds(t * TILE, TILE)
            c = [cs[b, d : d + 1, at] for d in range(3)]
            half = [0.5 * v * (1.0 - v) for v in c]
            for r0, r1 in ROWSETS:
                q = qx[b, r0:r1, at]
                if t == 0:
                    far = pltpu.roll(qx[sx, r0:r1, tx], rx, 1)
                else:
                    far = qx[b, r0:r1, pl.ds((t - 1) * TILE, TILE)]
                before = (
                    pltpu.roll(jnp.where(low, q, far), 64, 1),
                    jnp.where(y0, pltpu.roll(qx[sy, r0:r1, at], ry, 1), pltpu.roll(q, 8, 1)),
                    jnp.where(z0, pltpu.roll(qx[sz, r0:r1, at], rz, 1), pltpu.roll(q, 1, 1)),
                )
                rest = q
                for d in range(3):
                    m = jnp.maximum(jnp.minimum(q - before[d], q), 0.0)
                    flux = c[d] * q + half[d] * m
                    fluxes[d][b, r0:r1, at] = flux
                    rest = rest - flux
                q2[b, r0:r1, at] = rest
        return carry

    lax.fori_loop(0, oc, limit, 0)

    def step(b, carry):
        sx, tx, rx, sy, ry, sz, rz = sources(tab, b)
        for t in range(TILES):
            at = pl.ds(t * TILE, TILE)
            for r0, r1 in ROWSETS:
                if t == 0:
                    far = pltpu.roll(fx[sx, r0:r1, tx], rx, 1)
                else:
                    far = fx[b, r0:r1, pl.ds((t - 1) * TILE, TILE)]
                inx = pltpu.roll(jnp.where(low, fx[b, r0:r1, at], far), 64, 1)
                iny = jnp.where(
                    y0, pltpu.roll(fy[sy, r0:r1, at], ry, 1), pltpu.roll(fy[b, r0:r1, at], 8, 1)
                )
                inz = jnp.where(
                    z0, pltpu.roll(fz[sz, r0:r1, at], rz, 1), pltpu.roll(fz[b, r0:r1, at], 1, 1)
                )
                q2[b, r0:r1, at] = q2[b, r0:r1, at] + (inx + (iny + inz))
        return carry

    lax.fori_loop(0, oc, step, 0)
    outs = [pltpu.make_async_copy(q2, q2out, osems.at[0])]
    for side, refs in enumerate((ups, dns)):
        first = oc - HALF if side == 0 else 0
        for c in range(chunks):
            for i in range(CHUNK):
                block = first + c * CHUNK + i
                outs.append(
                    pltpu.make_async_copy(
                        q2.at[block, pl.ds(0, MAIN)],
                        refs[c].at[pl.ds(MAIN * i, MAIN)],
                        msems.at[side, c, i],
                    )
                )
                tails[side, c, 2 * i : 2 * i + 2, :] = q2[block, MAIN:BINS, :]
            outs.append(
                pltpu.make_async_copy(
                    tails.at[side, c],
                    refs[c].at[pl.ds(MAIN * CHUNK, 2 * CHUNK)],
                    msems.at[side, c, CHUNK],
                )
            )
    for copy in outs[1:]:
        copy.start()
    outs[0].start()
    for copy in outs:
        copy.wait()


def build_pairs(q, qp, pairs):
    qp[0:BINS, :] = q
    qp[BINS:ROWS, :] = jnp.zeros((ROWS - BINS, CELLS), F32)
    pending = []

    def emit(term):
        pending.append(term)
        if len(pending) % 2 == 0:
            at = 8 * (len(pending) - 2)
            tile = jnp.concatenate(pending[-2:], axis=0)
            pairs[at : at + 16, :] = tile.astype(jnp.bfloat16)

    def lead(i):
        return jnp.broadcast_to(qp[i : i + 1, :], (8, CELLS))

    def group(g):
        return qp[8 * g : 8 * g + 8, :]

    for a in range(7):
        for r in range(8):
            by = lead(8 * a + r)
            for b in range(a + 1, 8):
                emit(by * group(b))
    for e in (BINS - 2, BINS - 1):
        by = lead(e)
        for a in range(8):
            emit(by * group(a))
    for a in range(8):
        g = group(a)
        emit(g * g)
        for k in range(1, 5):
            emit(g * pltpu.roll(g, 8 - k, 0))
    tail = group(8)
    emit(tail * tail)
    emit(lead(BINS - 1) * tail)
    while len(pending) < GROUPS:
        emit(jnp.zeros((8, CELLS), F32))


def coalesce(count, load, slot_of, w, out, qps, pairs, res, sems):
    def copy_out(slot, buf):
        return pltpu.make_async_copy(res.at[buf], out.at[slot], sems.at[buf])

    def body(it, carry):
        first = 2 * it
        items = (first, jnp.minimum(first + 1, count - 1))
        values = [load(i) for i in items]

        @pl.when(it > 0)
        def _():
            for buf in range(2):
                copy_out(0, buf).wait()

        for buf in range(2):
            build_pairs(values[buf], qps[buf], pairs[buf])
        for buf in range(2):
            gain = jnp.dot(w[...], pairs[buf][...], preferred_element_type=F32)
            res[buf] = qps[buf][0:BINS, :] + gain
        copy_out(slot_of(items[0]), 0).start()

        @pl.when(first + 1 < count)
        def _():
            copy_out(slot_of(items[1]), 1).start()

        return carry

    trips = lax.div(count + 1, 2)
    lax.fori_loop(0, trips, body, 0)

    @pl.when(trips > 0)
    def _():
        copy_out(0, 0).wait()

    @pl.when((trips > 0) & (lax.rem(count, 2) == 0))
    def _():
        copy_out(0, 1).wait()


def ranges(tab):
    oc, nc, old, new = tab[T_OC], tab[T_NC], tab[T_OS], tab[T_NS]
    lo = jnp.clip(old - new, 0, nc)
    hi = jnp.clip(old + oc - new, lo, nc)
    return lo, hi, nc, new - old


def stay_kernel(capacity, tab, q2, w, out, qpa, qpb, pa, pb, res, zero, sems, zsem):
    lo, hi, nc, shift = ranges(tab)
    zero[...] = jnp.zeros_like(zero)

    def blank(slot):
        return pltpu.make_async_copy(zero, out.at[slot], zsem)

    def start(slot, carry):
        blank(slot).start()
        return carry

    def wait(slot, carry):
        blank(slot).wait()
        return carry

    lax.fori_loop(nc, capacity, start, 0)
    coalesce(
        hi - lo,
        lambda i: q2[i + lo + shift],
        lambda i: i + lo,
        w,
        out,
        (qpa, qpb),
        (pa, pb),
        res,
        sems,
    )
    lax.fori_loop(nc, capacity, wait, 0)


def come_kernel(c, tab, from_prev, from_next, w, old_out, out, qpa, qpb, pa, pb, res, src, tails, sems, lsems):
    lo, hi, nc, _ = ranges(tab)
    loads = []
    for side, ref in enumerate((from_prev, from_next)):
        for i in range(CHUNK):
            loads.append(
                pltpu.make_async_copy(
                    ref.at[pl.ds(MAIN * i, MAIN)],
                    src.at[side * CHUNK + i, pl.ds(0, MAIN)],
                    lsems.at[side, i],
                )
            )
        loads.append(
            pltpu.make_async_copy(
                ref.at[pl.ds(MAIN * CHUNK, 2 * CHUNK)], tails.at[side], lsems.at[side, CHUNK]
            )
        )
    for copy in loads:
        copy.start()
    for copy in loads:
        copy.wait()
    for side in range(2):
        for i in range(CHUNK):
            src[side * CHUNK + i, MAIN:BINS, :] = tails[side, 2 * i : 2 * i + 2, :]
    skip = jnp.clip(HALF - lo - c * CHUNK, 0, CHUNK)
    ups = CHUNK - skip
    downs = jnp.clip(nc - hi - c * CHUNK, 0, CHUNK)
    slot_up = c * CHUNK + skip - HALF + lo
    slot_dn = hi + c * CHUNK
    coalesce(
        ups + downs,
        lambda i: src[jnp.where(i < ups, i + skip, i - ups + CHUNK)],
        lambda i: jnp.where(i < ups, i + slot_up, i - ups + slot_dn),
        w,
        out,
        (qpa, qpb),
        (pa, pb),
        res,
        sems,
    )


def diagonal_picks():
    row = lax.broadcasted_iota(jnp.int32, (64, 40), 0)
    col = lax.broadcasted_iota(jnp.int32, (64, 40), 1)
    i, j, k, s = row // 8, row % 8, col // 8, col % 8
    t = (s + k) % 8
    direct = (i == s) & (j == t)
    mirror = (i == t) & (j == s) & (k > 0) & (k < 4)
    return (direct | mirror).astype(jnp.bfloat16)


def folded_kernel(kernel):
    cube = kernel.reshape(BINS, BINS, BINS).astype(F32)
    both = cube + jnp.swapaxes(cube, 1, 2)
    a, b = BINS - 2, BINS - 1
    parts = [both[:, 8 * g : 8 * g + 8, 8 * g + 8 : a].reshape(BINS, -1) for g in range(7)]
    parts += [both[:, a, :a], both[:, b, :a]]
    narrow = kernel.reshape(BINS, BINS, BINS)
    spans = [slice(8 * g, 8 * g + 8) for g in range(8)]
    blocks = jnp.stack([narrow[:, at, at] for at in spans], axis=1).reshape(BINS * 8, 64)
    pick = lax.dot(blocks, diagonal_picks(), preferred_element_type=F32)
    parts.append(pick.reshape(BINS, 8 * 40))
    zero = jnp.zeros((BINS, 6), F32)
    parts += [cube[:, a, a][:, None], cube[:, b, b][:, None], zero]
    parts += [both[:, a, b][:, None], jnp.zeros((BINS, 7), F32)]
    width = sum(p.shape[1] for p in parts)
    parts.append(jnp.zeros((BINS, KDIM - width), F32))
    return jnp.concatenate([p.astype(jnp.bfloat16) for p in parts], axis=1)


def on_device(n, spectra, courant, kernel, old_count, new_count, upwind):
    capacity = spectra.shape[0]
    shape = jax.ShapeDtypeStruct
    vmem = pl.BlockSpec(memory_space=pltpu.VMEM)
    smem = pl.BlockSpec(memory_space=pltpu.SMEM)
    hbm = pl.BlockSpec(memory_space=pl.ANY)
    params = pltpu.CompilerParams(vmem_limit_bytes=VMEM_LIMIT)
    blocks = shape((capacity, BINS, CELLS), F32)
    chunk = shape((CHUNK * BINS, CELLS), F32)
    chunks = HALF // CHUNK
    wide = pltpu.VMEM((capacity + EXTRA, BINS, CELLS), F32)
    dma = pltpu.SemaphoreType.DMA

    def cost(flops, nbytes):
        return pl.CostEstimate(flops=flops, bytes_accessed=nbytes, transcendentals=0)

    upw = jnp.swapaxes(upwind, 0, 1)
    sends, up, dn, cs = pl.pallas_call(
        functools.partial(faces_kernel, n, capacity),
        out_shape=(
            shape((S_LIST + 32,), jnp.int32),
            shape((BINS, PACK), F32),
            shape((BINS, PACK), F32),
            shape((capacity, 3, CELLS), F32),
        ),
        in_specs=[smem, smem, smem, vmem, vmem],
        out_specs=(smem, vmem, vmem, vmem),
        compiler_params=params,
        name="faces",
    )(old_count, new_count, upw, spectra, jnp.swapaxes(courant, 0, 1))

    def along(value, step, ring):
        route = [(i, i + step) for i in range(n)]
        if ring:
            route = [(i, j % n) for i, j in route]
        return lax.ppermute(value, "blocks", [(i, j) for i, j in route if 0 <= j < n])

    from_prev, from_next = along(up, 1, True), along(dn, -1, True)
    tab = pl.pallas_call(
        functools.partial(plan_kernel, n, capacity),
        out_shape=shape((T_SRC + 8 * capacity,), jnp.int32),
        in_specs=[smem] * 4,
        out_specs=smem,
        cost_estimate=cost(1000000, 1000000),
        name="plan",
    )(sends, old_count, new_count, upw)
    weights = folded_kernel(kernel)
    packed = shape((BINS, 2 * PACK), F32)
    q1, up, dn = pl.pallas_call(
        functools.partial(first_kernel, capacity),
        out_shape=(blocks, packed, packed),
        in_specs=[smem, smem, hbm, hbm, hbm, hbm],
        out_specs=(vmem, vmem, vmem),
        scratch_shapes=[
            wide,
            pltpu.VMEM((capacity + EXTRA, 3, CELLS), F32),
            dma,
            dma((9,)),
        ],
        compiler_params=params,
        name="first",
    )(tab, sends, spectra, cs, from_prev, from_next)
    from_prev, from_next = along(up, 1, True), along(dn, -1, True)
    q1, weights = lax.optimization_barrier((q1, weights))
    q2, *moved = pl.pallas_call(
        functools.partial(second_kernel, capacity),
        out_shape=[blocks] + [chunk] * (2 * chunks),
        in_specs=[smem, hbm, vmem, hbm, hbm],
        out_specs=[hbm] * (1 + 2 * chunks),
        scratch_shapes=[
            wide,
            wide,
            wide,
            wide,
            pltpu.VMEM((capacity, BINS, CELLS), F32),
            pltpu.VMEM((2, chunks, 2 * CHUNK, CELLS), F32),
            dma,
            dma((8,)),
            dma((8,)),
            dma((1,)),
            dma((2, chunks, CHUNK + 1)),
        ],
        compiler_params=params,
        name="second",
    )(tab, q1, cs, from_prev, from_next)
    arrived = [
        (along(moved[c], 1, False), along(moved[chunks + c], -1, False)) for c in range(chunks)
    ]
    buffers = [
        pltpu.VMEM((ROWS, CELLS), F32),
        pltpu.VMEM((ROWS, CELLS), F32),
        pltpu.VMEM((KDIM, CELLS), jnp.bfloat16),
        pltpu.VMEM((KDIM, CELLS), jnp.bfloat16),
        pltpu.VMEM((2, BINS, CELLS), F32),
    ]
    work = 2 * BINS * KDIM * CELLS
    updated = pl.pallas_call(
        functools.partial(stay_kernel, capacity),
        out_shape=blocks,
        in_specs=[smem, vmem, vmem],
        out_specs=hbm,
        scratch_shapes=buffers + [pltpu.VMEM((BINS, CELLS), F32), dma((2,)), dma],
        compiler_params=params,
        cost_estimate=cost(24 * work, 12 * 1024 * 1024),
        name="stay",
    )(tab, q2, weights)
    for c in range(chunks):
        updated = pl.pallas_call(
            functools.partial(come_kernel, c),
            out_shape=blocks,
            in_specs=[smem, hbm, hbm, vmem, hbm],
            out_specs=hbm,
            input_output_aliases={4: 0},
            scratch_shapes=buffers
            + [
                pltpu.VMEM((2 * CHUNK, BINS, CELLS), F32),
                pltpu.VMEM((2, 2 * CHUNK, CELLS), F32),
                dma((2,)),
                dma((2, CHUNK + 1)),
            ],
            compiler_params=params,
            cost_estimate=cost(8 * work, 4 * 1024 * 1024),
            name=f"come{c}",
        )(tab, *arrived[c], weights, updated)
    return updated


def solution(mesh):
    in_specs = (P("blocks", None, None), P("blocks", None, None), P(), P(), P(), P())
    out_specs = P("blocks", None, None)
    return jax.shard_map(
        functools.partial(on_device, mesh.shape["blocks"]),
        mesh=mesh,
        in_specs=in_specs,
        out_specs=out_specs,
        check_vma=False,
    )
```

```python
import functools

import jax
import jax.numpy as jnp
from jax import lax
from jax.experimental import pallas as pl
from jax.experimental.pallas import tpu as pltpu
from jax.sharding import PartitionSpec as P

HALF = 12
BINS = 66
EDGE = 8
CELLS = 512
TILE = 128
TILES = CELLS // TILE
YZ = 6
XFACES = HALF * 64
PACK = XFACES + 2 * CELLS
EXTRA = 8
ROWS = 72
GROUPS = 288
KDIM = 8 * GROUPS
CHUNK = 6
MAIN = 64
TAIL = 16
STRIDES = (64, 8, 1)
ROWSETS = ((0, 32), (32, 64), (64, 66))
VMEM_LIMIT = 63 * 1024 * 1024
F32 = jnp.float32

T_OC, T_NC, T_OS, T_NS = 0, 1, 2, 3
T_SRC = 8
S_COUNT = 0
S_LIST = 8


def position(n, old, new):
    me = lax.axis_index("blocks")

    def total(ref):
        return lax.fori_loop(0, me, lambda i, s: s + ref[i], jnp.int32(0))

    return total(old), total(new), old[me], new[me]


def lane_coord(direction):
    lane = lax.broadcasted_iota(jnp.int32, (1, TILE), 1)
    return (lane // STRIDES[direction]) % EDGE


def low_half():
    return lax.broadcasted_iota(jnp.int32, (1, TILE), 1) < 64


def send_table(capacity, old_start, oc, up, sends):
    zero = jnp.int32(0)
    end_run = lax.rem(old_start + oc, HALF)
    start_run = lax.rem(old_start, HALF)
    for d in (1, 2):

        def link(t, counts):
            s_up, s_dn = counts
            u = up[d, HALF + t] - HALF
            cross = (t >= end_run) & (u < end_run)

            @pl.when(cross)
            def _():
                sends[S_LIST + (d - 1) * 8 + s_up] = jnp.clip(oc - end_run + u, 0, capacity - 1)

            s_up = s_up + cross.astype(jnp.int32)
            cross = (t < start_run) & (u >= start_run)

            @pl.when(cross)
            def _():
                sends[S_LIST + 16 + (d - 1) * 8 + s_dn] = jnp.clip(u - start_run, 0, capacity - 1)

            return s_up, s_dn + cross.astype(jnp.int32)

        s_up, s_dn = lax.fori_loop(0, HALF, link, (zero, zero))
        sends[S_COUNT + d - 1] = jnp.minimum(s_up, YZ)
        sends[S_COUNT + 2 + d - 1] = jnp.minimum(s_dn, YZ)


def plan_kernel(n, capacity, sends, old, new, up, tab):
    old_start, new_start, oc, nc = position(n, old, new)
    tab[T_OC] = oc
    tab[T_NC] = nc
    tab[T_OS] = old_start
    tab[T_NS] = new_start
    tab[T_OC + 4] = sends[S_COUNT]
    end_run = lax.rem(old_start + oc, HALF)
    start_run = lax.rem(old_start, HALF)
    zero = jnp.int32(0)

    def block_src(b, pos):
        at = T_SRC + 8 * b
        u = b + up[0, HALF + pos] - HALF - pos
        above = u >= oc
        remote = above | (u < 0)
        j = jnp.where(above, u - oc, u + HALF)
        base = capacity + jnp.where(above, 4, 0)
        tab[at] = jnp.where(remote, base + (j >> 3), u)
        tab[at + 1] = jnp.where(remote, ((j & 7) >> 1) * TILE, CELLS - TILE)
        tab[at + 2] = jnp.where(remote & ((j & 1) == 0), 64, 0)
        for d in (1, 2):
            tab[at + 1 + 2 * d] = jnp.clip(b + up[d, HALF + pos] - HALF - pos, 0, capacity - 1)
            tab[at + 2 + 2 * d] = TILE - STRIDES[d] * (EDGE - 1)
        return jnp.where(pos == HALF - 1, 0, pos + 1)

    lax.fori_loop(0, capacity, block_src, start_run)

    for d in (1, 2):

        def link(t, counts):
            r_up, r_dn = counts
            u = up[d, HALF + t] - HALF

            def put(b, side, k):
                at = T_SRC + 8 * jnp.clip(b, 0, capacity - 1) + 1 + 2 * d
                tab[at] = capacity + 4 * side + 1 + d
                tab[at + 1] = (TILE - STRIDES[d] * k) & (TILE - 1)

            cross = (t < end_run) & (u >= end_run)

            @pl.when(cross)
            def _():
                put(oc - end_run + t, 1, r_dn)

            r_dn = r_dn + cross.astype(jnp.int32)
            cross = (t >= start_run) & (u < start_run)

            @pl.when(cross)
            def _():
                put(t - start_run, 0, r_up)

            return r_up + cross.astype(jnp.int32), r_dn

        lax.fori_loop(0, HALF, link, (zero, zero))


def pack(oc, sends, field, outs):
    low = low_half()
    coords = [lane_coord(d) for d in range(3)]
    last = pl.ds(CELLS - TILE, TILE)

    def faces(jp, carry):
        for side in range(2):
            first = (oc - HALF if side == 0 else 0) + 2 * jp
            a = field(first, 0, last)
            b = field(first + 1, 0, last)
            for part in range(len(a)):
                lane = pl.multiple_of(part * PACK + jp * TILE, TILE)
                outs[side][:, pl.ds(lane, TILE)] = jnp.where(low, pltpu.roll(a[part], 64, 1), b[part])
        return carry

    lax.fori_loop(0, HALF // 2, faces, 0)
    for side in range(2):
        for d in (1, 2):

            def cross(k, carry, side=side, d=d):
                block = sends[S_LIST + side * 16 + (d - 1) * 8 + k]
                shift = TILE - STRIDES[d] * (EDGE - 1) + STRIDES[d] * k
                for t in range(TILES):
                    values = field(block, d, pl.ds(t * TILE, TILE))
                    for part, value in enumerate(values):
                        lane = part * PACK + XFACES + (d - 1) * CELLS + t * TILE
                        at = pl.ds(lane, TILE)
                        keep = outs[side][:, at]
                        outs[side][:, at] = jnp.where(coords[d] == k, pltpu.roll(value, shift, 1), keep)
                return carry

            lax.fori_loop(0, sends[S_COUNT + side * 2 + d - 1], cross, 0)


def faces_kernel(n, capacity, old, new, upw, q0, speeds, sends, up, dn, cs):
    old_start, _, oc, _ = position(n, old, new)
    send_table(capacity, old_start, oc, upw, sends)
    for b0 in range(0, capacity, 8):
        b1 = min(b0 + 8, capacity)
        for t in range(TILES):
            at = pl.ds(t * TILE, TILE)
            cs[b0:b1, :, at] = jnp.swapaxes(speeds[:, b0:b1, at], 0, 1)

    def field(block, d, lanes):
        return (q0[block, :, lanes] * cs[block, d : d + 1, lanes],)

    pack(oc, sends, field, (up, dn))


def spread(capacity, packets, part, targets, sems):
    copies = []
    for side, packet in enumerate(packets):
        base = part * PACK
        slot = capacity + 4 * side
        pieces = (
            (0, 0, CELLS),
            (1, CELLS, XFACES - CELLS),
            (2, XFACES, CELLS),
            (3, XFACES + CELLS, CELLS),
        )
        for i, (sub, lane, width) in enumerate(pieces):
            target = targets[max(sub - 1, 0)]
            copies.append(
                pltpu.make_async_copy(
                    packet.at[:, pl.ds(base + lane, width)],
                    target.at[slot + sub, :, pl.ds(0, width)],
                    sems.at[4 * side + i],
                )
            )
    return copies


def sources(tab, b):
    at = T_SRC + 8 * b
    sx, tx, rx, sy, ry, sz, rz = [tab[at + i] for i in range(7)]
    return sx, pl.ds(pl.multiple_of(tx, TILE), TILE), rx, sy, ry, sz, rz


def first_kernel(capacity, tab, sends, q0, cs, from_prev, from_next, q1, up, dn, qx, cx, sem, sems):
    load = pltpu.make_async_copy(q0, qx.at[pl.ds(0, capacity)], sem)
    load.start()
    copies = spread(capacity, (from_prev, from_next), 0, (qx, qx, qx), sems)
    for copy in copies:
        copy.start()
    table = pltpu.make_async_copy(cs, cx.at[pl.ds(0, capacity)], sems.at[8])
    table.start()
    copies.append(table)
    for i in range(EXTRA):
        cx[capacity + i] = jnp.ones((3, CELLS), F32)
    for copy in copies:
        copy.wait()
    load.wait()
    low = low_half()
    y0, z0 = lane_coord(1) == 0, lane_coord(2) == 0
    oc = tab[T_OC]

    def step(b, carry):
        sx, tx, rx, sy, ry, sz, rz = sources(tab, b)
        before = None
        for t in range(TILES):
            at = pl.ds(t * TILE, TILE)
            c = [cx[b, d : d + 1, at] for d in range(3)]
            keep = 1.0 - c[0] - c[1] - c[2]
            cuy, cuz = cx[sy, 1:2, at], cx[sz, 2:3, at]
            if t == 0:
                cux = cx[sx, 0:1, tx]
            else:
                cm = jnp.where(low, c[0], before)
            for r0, r1 in ROWSETS:
                q = qx[b, r0:r1, at]
                if t == 0:
                    far = pltpu.roll(qx[sx, r0:r1, tx] * cux, rx, 1)
                    mixed = jnp.where(low, q * c[0], far)
                else:
                    mixed = jnp.where(low, q, qx[b, r0:r1, pl.ds((t - 1) * TILE, TILE)]) * cm
                inx = pltpu.roll(mixed, 64, 1)
                iny = jnp.where(
                    y0, pltpu.roll(qx[sy, r0:r1, at] * cuy, ry, 1), pltpu.roll(q * c[1], 8, 1)
                )
                inz = jnp.where(
                    z0, pltpu.roll(qx[sz, r0:r1, at] * cuz, rz, 1), pltpu.roll(q * c[2], 1, 1)
                )
                q1[b, r0:r1, at] = q * keep + (inx + (iny + inz))
            before = c[0]
        return carry

    lax.fori_loop(0, oc, step, 0)

    def field(block, d, lanes):
        q = q1[block, :, lanes]
        c = cx[block, d : d + 1, lanes]
        m = q - pltpu.roll(q, STRIDES[d], 1)
        m = jnp.maximum(jnp.minimum(m, q), 0.0)
        return c * q + (0.5 * c * (1.0 - c)) * m, q

    pack(oc, sends, field, (up, dn))


def second_kernel(
    capacity, tab, q1, cs, from_prev, from_next, q2out, *rest
):
    chunks = HALF // CHUNK
    ups, dns = rest[:chunks], rest[chunks : 2 * chunks]
    qx, fx, fy, fz, q2, tails, sem, lsems, fsems, osems, msems = rest[2 * chunks :]
    fluxes = (fx, fy, fz)
    packets = (from_prev, from_next)
    load = pltpu.make_async_copy(q1, qx.at[pl.ds(0, capacity)], sem)
    load.start()
    copies = spread(capacity, packets, 1, (qx, qx, qx), lsems)
    copies += spread(capacity, packets, 0, fluxes, fsems)
    for copy in copies:
        copy.start()
    for copy in copies:
        copy.wait()
    load.wait()
    low = low_half()
    y0, z0 = lane_coord(1) == 0, lane_coord(2) == 0
    oc = tab[T_OC]

    def limit(b, carry):
        sx, tx, rx, sy, ry, sz, rz = sources(tab, b)
        for t in range(TILES):
            at = pl.ds(t * TILE, TILE)
            c = [cs[b, d : d + 1, at] for d in range(3)]
            half = [0.5 * v * (1.0 - v) for v in c]
            for r0, r1 in ROWSETS:
                q = qx[b, r0:r1, at]
                if t == 0:
                    far = pltpu.roll(qx[sx, r0:r1, tx], rx, 1)
                else:
                    far = qx[b, r0:r1, pl.ds((t - 1) * TILE, TILE)]
                before = (
                    pltpu.roll(jnp.where(low, q, far), 64, 1),
                    jnp.where(y0, pltpu.roll(qx[sy, r0:r1, at], ry, 1), pltpu.roll(q, 8, 1)),
                    jnp.where(z0, pltpu.roll(qx[sz, r0:r1, at], rz, 1), pltpu.roll(q, 1, 1)),
                )
                rest = q
                for d in range(3):
                    m = jnp.maximum(jnp.minimum(q - before[d], q), 0.0)
                    flux = c[d] * q + half[d] * m
                    fluxes[d][b, r0:r1, at] = flux
                    rest = rest - flux
                q2[b, r0:r1, at] = rest
        return carry

    lax.fori_loop(0, oc, limit, 0)

    def step(b, carry):
        sx, tx, rx, sy, ry, sz, rz = sources(tab, b)
        for t in range(TILES):
            at = pl.ds(t * TILE, TILE)
            for r0, r1 in ROWSETS:
                if t == 0:
                    far = pltpu.roll(fx[sx, r0:r1, tx], rx, 1)
                else:
                    far = fx[b, r0:r1, pl.ds((t - 1) * TILE, TILE)]
                inx = pltpu.roll(jnp.where(low, fx[b, r0:r1, at], far), 64, 1)
                iny = jnp.where(
                    y0, pltpu.roll(fy[sy, r0:r1, at], ry, 1), pltpu.roll(fy[b, r0:r1, at], 8, 1)
                )
                inz = jnp.where(
                    z0, pltpu.roll(fz[sz, r0:r1, at], rz, 1), pltpu.roll(fz[b, r0:r1, at], 1, 1)
                )
                q2[b, r0:r1, at] = q2[b, r0:r1, at] + (inx + (iny + inz))
        return carry

    lax.fori_loop(0, oc, step, 0)
    outs = [pltpu.make_async_copy(q2, q2out, osems.at[0])]
    for side, refs in enumerate((ups, dns)):
        first = oc - HALF if side == 0 else 0
        for c in range(chunks):
            for i in range(CHUNK):
                block = first + c * CHUNK + i
                outs.append(
                    pltpu.make_async_copy(
                        q2.at[block, pl.ds(0, MAIN)],
                        refs[c].at[pl.ds(MAIN * i, MAIN)],
                        msems.at[side, c, i],
                    )
                )
                tails[side, c, 2 * i : 2 * i + 2, :] = q2[block, MAIN:BINS, :]
            outs.append(
                pltpu.make_async_copy(
                    tails.at[side, c],
                    refs[c].at[pl.ds(MAIN * CHUNK, TAIL)],
                    msems.at[side, c, CHUNK],
                )
            )
    for copy in outs[1:]:
        copy.start()
    outs[0].start()
    for copy in outs:
        copy.wait()


def build_pairs(q, qp, pairs):
    qp[0:BINS, :] = q
    qp[BINS:ROWS, :] = jnp.zeros((ROWS - BINS, CELLS), F32)
    pending = []

    def emit(term):
        pending.append(term)
        if len(pending) % 2 == 0:
            at = 8 * (len(pending) - 2)
            tile = jnp.concatenate(pending[-2:], axis=0)
            pairs[at : at + 16, :] = tile.astype(jnp.bfloat16)

    def lead(i):
        return jnp.broadcast_to(qp[i : i + 1, :], (8, CELLS))

    def group(g):
        return qp[8 * g : 8 * g + 8, :]

    for a in range(7):
        for r in range(8):
            by = lead(8 * a + r)
            for b in range(a + 1, 8):
                emit(by * group(b))
    for e in (BINS - 2, BINS - 1):
        by = lead(e)
        for a in range(8):
            emit(by * group(a))
    for a in range(8):
        g = group(a)
        emit(g * g)
        for k in range(1, 5):
            emit(g * pltpu.roll(g, 8 - k, 0))
    tail = group(8)
    emit(tail * tail)
    emit(lead(BINS - 1) * tail)
    while len(pending) < GROUPS:
        emit(jnp.zeros((8, CELLS), F32))


def coalesce(count, load, slot_of, w, out, qps, pairs, res, sems):
    def copy_out(slot, buf):
        return pltpu.make_async_copy(res.at[buf], out.at[slot], sems.at[buf])

    def body(it, carry):
        first = 2 * it
        items = (first, jnp.minimum(first + 1, count - 1))
        values = [load(i) for i in items]

        @pl.when(it > 0)
        def _():
            for buf in range(2):
                copy_out(0, buf).wait()

        for buf in range(2):
            build_pairs(values[buf], qps[buf], pairs[buf])
        for buf in range(2):
            gain = jnp.dot(w[...], pairs[buf][...], preferred_element_type=F32)
            res[buf] = qps[buf][0:BINS, :] + gain
        copy_out(slot_of(items[0]), 0).start()

        @pl.when(first + 1 < count)
        def _():
            copy_out(slot_of(items[1]), 1).start()

        return carry

    trips = lax.div(count + 1, 2)
    lax.fori_loop(0, trips, body, 0)

    @pl.when(trips > 0)
    def _():
        copy_out(0, 0).wait()

    @pl.when((trips > 0) & (lax.rem(count, 2) == 0))
    def _():
        copy_out(0, 1).wait()


def ranges(tab):
    oc, nc, old, new = tab[T_OC], tab[T_NC], tab[T_OS], tab[T_NS]
    lo = jnp.clip(old - new, 0, nc)
    hi = jnp.clip(old + oc - new, lo, nc)
    return lo, hi, nc, new - old


def stay_kernel(capacity, tab, q2, w, out, qpa, qpb, pa, pb, res, zero, sems, zsem):
    lo, hi, nc, shift = ranges(tab)
    zero[...] = jnp.zeros_like(zero)

    def blank(slot):
        return pltpu.make_async_copy(zero, out.at[slot], zsem)

    def start(slot, carry):
        blank(slot).start()
        return carry

    def wait(slot, carry):
        blank(slot).wait()
        return carry

    lax.fori_loop(nc, capacity, start, 0)
    coalesce(
        hi - lo,
        lambda i: q2[i + lo + shift],
        lambda i: i + lo,
        w,
        out,
        (qpa, qpb),
        (pa, pb),
        res,
        sems,
    )
    lax.fori_loop(nc, capacity, wait, 0)


def come_kernel(c, tab, from_prev, from_next, w, old_out, out, qpa, qpb, pa, pb, res, src, tails, sems, lsems):
    lo, hi, nc, _ = ranges(tab)
    loads = []
    for side, ref in enumerate((from_prev, from_next)):
        for i in range(CHUNK):
            loads.append(
                pltpu.make_async_copy(
                    ref.at[pl.ds(MAIN * i, MAIN)],
                    src.at[side * CHUNK + i, pl.ds(0, MAIN)],
                    lsems.at[side, i],
                )
            )
        loads.append(
            pltpu.make_async_copy(
                ref.at[pl.ds(MAIN * CHUNK, TAIL)], tails.at[side], lsems.at[side, CHUNK]
            )
        )
    for copy in loads:
        copy.start()
    for copy in loads:
        copy.wait()
    for side in range(2):
        for i in range(CHUNK):
            src[side * CHUNK + i, MAIN:BINS, :] = tails[side, 2 * i : 2 * i + 2, :]
    skip = jnp.clip(HALF - lo - c * CHUNK, 0, CHUNK)
    ups = CHUNK - skip
    downs = jnp.clip(nc - hi - c * CHUNK, 0, CHUNK)
    slot_up = c * CHUNK + skip - HALF + lo
    slot_dn = hi + c * CHUNK
    coalesce(
        ups + downs,
        lambda i: src[jnp.where(i < ups, i + skip, i - ups + CHUNK)],
        lambda i: jnp.where(i < ups, i + slot_up, i - ups + slot_dn),
        w,
        out,
        (qpa, qpb),
        (pa, pb),
        res,
        sems,
    )


def diagonal_picks():
    row = lax.broadcasted_iota(jnp.int32, (64, 40), 0)
    col = lax.broadcasted_iota(jnp.int32, (64, 40), 1)
    i, j, k, s = row // 8, row % 8, col // 8, col % 8
    t = (s + k) % 8
    direct = (i == s) & (j == t)
    mirror = (i == t) & (j == s) & (k > 0) & (k < 4)
    return (direct | mirror).astype(jnp.bfloat16)


def folded_kernel(narrow):
    cube = narrow.astype(F32)
    both = cube + jnp.swapaxes(cube, 1, 2)
    a, b = BINS - 2, BINS - 1
    parts = [both[:, 8 * g : 8 * g + 8, 8 * g + 8 : a].reshape(BINS, -1) for g in range(7)]
    parts += [both[:, a, :a], both[:, b, :a]]
    spans = [slice(8 * g, 8 * g + 8) for g in range(8)]
    blocks = jnp.stack([narrow[:, at, at] for at in spans], axis=1).reshape(BINS * 8, 64)
    pick = lax.dot(blocks, diagonal_picks(), preferred_element_type=F32)
    parts.append(pick.reshape(BINS, 8 * 40))
    zero = jnp.zeros((BINS, 6), F32)
    parts += [cube[:, a, a][:, None], cube[:, b, b][:, None], zero]
    parts += [both[:, a, b][:, None], jnp.zeros((BINS, 7), F32)]
    width = sum(p.shape[1] for p in parts)
    parts.append(jnp.zeros((BINS, KDIM - width), F32))
    return jnp.concatenate([p.astype(jnp.bfloat16) for p in parts], axis=1)


def on_device(n, spectra, courant, kernel, old_count, new_count, upwind):
    capacity = spectra.shape[0]
    shape = jax.ShapeDtypeStruct
    vmem = pl.BlockSpec(memory_space=pltpu.VMEM)
    smem = pl.BlockSpec(memory_space=pltpu.SMEM)
    hbm = pl.BlockSpec(memory_space=pl.ANY)
    params = pltpu.CompilerParams(vmem_limit_bytes=VMEM_LIMIT)
    blocks = shape((capacity, BINS, CELLS), F32)
    chunk = shape((CHUNK * MAIN + TAIL, CELLS), F32)
    chunks = HALF // CHUNK
    wide = pltpu.VMEM((capacity + EXTRA, BINS, CELLS), F32)
    dma = pltpu.SemaphoreType.DMA

    def cost(flops, nbytes):
        return pl.CostEstimate(flops=flops, bytes_accessed=nbytes, transcendentals=0)

    upw = jnp.swapaxes(upwind, 0, 1)
    sends, up, dn, cs = pl.pallas_call(
        functools.partial(faces_kernel, n, capacity),
        out_shape=(
            shape((S_LIST + 32,), jnp.int32),
            shape((BINS, PACK), F32),
            shape((BINS, PACK), F32),
            shape((capacity, 3, CELLS), F32),
        ),
        in_specs=[smem, smem, smem, vmem, vmem],
        out_specs=(smem, vmem, vmem, vmem),
        compiler_params=params,
        name="faces",
    )(old_count, new_count, upw, spectra, jnp.swapaxes(courant, 0, 1))

    def along(value, step, ring):
        route = [(i, i + step) for i in range(n)]
        if ring:
            route = [(i, j % n) for i, j in route]
        return lax.ppermute(value, "blocks", [(i, j) for i, j in route if 0 <= j < n])

    from_prev, from_next = along(up, 1, True), along(dn, -1, True)
    tab = pl.pallas_call(
        functools.partial(plan_kernel, n, capacity),
        out_shape=shape((T_SRC + 8 * capacity,), jnp.int32),
        in_specs=[smem] * 4,
        out_specs=smem,
        cost_estimate=cost(1000000, 1000000),
        name="plan",
    )(sends, old_count, new_count, upw)
    cube = kernel.reshape(BINS, BINS, BINS)
    packed = shape((BINS, 2 * PACK), F32)
    q1, up, dn = pl.pallas_call(
        functools.partial(first_kernel, capacity),
        out_shape=(blocks, packed, packed),
        in_specs=[smem, smem, hbm, hbm, hbm, hbm],
        out_specs=(vmem, vmem, vmem),
        scratch_shapes=[
            wide,
            pltpu.VMEM((capacity + EXTRA, 3, CELLS), F32),
            dma,
            dma((9,)),
        ],
        compiler_params=params,
        name="first",
    )(tab, sends, spectra, cs, from_prev, from_next)
    from_prev, from_next = along(up, 1, True), along(dn, -1, True)
    q1, cube = lax.optimization_barrier((q1, cube))
    q1, weights = lax.optimization_barrier((q1, folded_kernel(cube)))
    q2, *moved = pl.pallas_call(
        functools.partial(second_kernel, capacity),
        out_shape=[blocks] + [chunk] * (2 * chunks),
        in_specs=[smem, hbm, vmem, hbm, hbm],
        out_specs=[hbm] * (1 + 2 * chunks),
        scratch_shapes=[
            wide,
            wide,
            wide,
            wide,
            pltpu.VMEM((capacity, BINS, CELLS), F32),
            pltpu.VMEM((2, chunks, TAIL, CELLS), F32),
            dma,
            dma((8,)),
            dma((8,)),
            dma((1,)),
            dma((2, chunks, CHUNK + 1)),
        ],
        compiler_params=params,
        name="second",
    )(tab, q1, cs, from_prev, from_next)
    arrived = [
        (along(moved[c], 1, False), along(moved[chunks + c], -1, False)) for c in range(chunks)
    ]
    buffers = [
        pltpu.VMEM((ROWS, CELLS), F32),
        pltpu.VMEM((ROWS, CELLS), F32),
        pltpu.VMEM((KDIM, CELLS), jnp.bfloat16),
        pltpu.VMEM((KDIM, CELLS), jnp.bfloat16),
        pltpu.VMEM((2, BINS, CELLS), F32),
    ]
    work = 2 * BINS * KDIM * CELLS
    updated = pl.pallas_call(
        functools.partial(stay_kernel, capacity),
        out_shape=blocks,
        in_specs=[smem, vmem, vmem],
        out_specs=hbm,
        scratch_shapes=buffers + [pltpu.VMEM((BINS, CELLS), F32), dma((2,)), dma],
        compiler_params=params,
        cost_estimate=cost(24 * work, 12 * 1024 * 1024),
        name="stay",
    )(tab, q2, weights)
    for c in range(chunks):
        updated = pl.pallas_call(
            functools.partial(come_kernel, c),
            out_shape=blocks,
            in_specs=[smem, hbm, hbm, vmem, hbm],
            out_specs=hbm,
            input_output_aliases={4: 0},
            scratch_shapes=buffers
            + [
                pltpu.VMEM((2 * CHUNK, BINS, CELLS), F32),
                pltpu.VMEM((2, TAIL, CELLS), F32),
                dma((2,)),
                dma((2, CHUNK + 1)),
            ],
            compiler_params=params,
            cost_estimate=cost(2 * CHUNK * work, 4 * 1024 * 1024),
            name=f"come{c}",
        )(tab, *arrived[c], weights, updated)
    return updated


def solution(mesh):
    in_specs = (P("blocks", None, None), P("blocks", None, None), P(), P(), P(), P())
    out_specs = P("blocks", None, None)
    return jax.shard_map(
        functools.partial(on_device, mesh.shape["blocks"]),
        mesh=mesh,
        in_specs=in_specs,
        out_specs=out_specs,
        check_vma=False,
    )
```

```python
import functools

import jax
import jax.numpy as jnp
from jax import lax
from jax.experimental import pallas as pl
from jax.experimental.pallas import tpu as pltpu
from jax.sharding import PartitionSpec as P

HALF = 12
BINS = 66
EDGE = 8
CELLS = 512
TILE = 128
TILES = CELLS // TILE
YZ = 6
XFACES = HALF * 64
PACK = XFACES + 2 * CELLS
PACKED = 8
EXTRA = PACKED + 4 * YZ
ROWS = 72
GROUPS = 288
KDIM = 8 * GROUPS
CHUNK = 6
MAIN = 64
TAIL = 16
STRIDES = (64, 8, 1)
ROWSETS = ((0, 32), (32, 64), (64, 66))
VMEM_LIMIT = 63 * 1024 * 1024
F32 = jnp.float32

T_OC, T_NC, T_OS, T_NS = 0, 1, 2, 3
T_GOT = 4
T_SRC = 8
S_COUNT = 0
S_LIST = 8


def position(n, old, new):
    me = lax.axis_index("blocks")

    def total(ref):
        return lax.fori_loop(0, me, lambda i, s: s + ref[i], jnp.int32(0))

    return total(old), total(new), old[me], new[me]


def lane_coord(direction):
    lane = lax.broadcasted_iota(jnp.int32, (1, TILE), 1)
    return (lane // STRIDES[direction]) % EDGE


def low_half():
    return lax.broadcasted_iota(jnp.int32, (1, TILE), 1) < 64


def send_table(capacity, old_start, oc, up, sends):
    zero = jnp.int32(0)
    end_run = lax.rem(old_start + oc, HALF)
    start_run = lax.rem(old_start, HALF)
    for d in (1, 2):

        def link(t, counts):
            s_up, s_dn = counts
            u = up[d, HALF + t] - HALF
            cross = (t >= end_run) & (u < end_run)

            @pl.when(cross)
            def _():
                sends[S_LIST + (d - 1) * 8 + s_up] = jnp.clip(oc - end_run + u, 0, capacity - 1)

            s_up = s_up + cross.astype(jnp.int32)
            cross = (t < start_run) & (u >= start_run)

            @pl.when(cross)
            def _():
                sends[S_LIST + 16 + (d - 1) * 8 + s_dn] = jnp.clip(u - start_run, 0, capacity - 1)

            return s_up, s_dn + cross.astype(jnp.int32)

        s_up, s_dn = lax.fori_loop(0, HALF, link, (zero, zero))
        sends[S_COUNT + d - 1] = jnp.minimum(s_up, YZ)
        sends[S_COUNT + 2 + d - 1] = jnp.minimum(s_dn, YZ)


def plan_kernel(n, capacity, sends, old, new, up, tab):
    old_start, new_start, oc, nc = position(n, old, new)
    tab[T_OC] = oc
    tab[T_NC] = nc
    tab[T_OS] = old_start
    tab[T_NS] = new_start
    tab[T_GOT] = sends[S_COUNT]
    end_run = lax.rem(old_start + oc, HALF)
    start_run = lax.rem(old_start, HALF)
    zero = jnp.int32(0)

    def block_src(b, pos):
        at = T_SRC + 8 * b
        u = b + up[0, HALF + pos] - HALF - pos
        above = u >= oc
        remote = above | (u < 0)
        j = jnp.where(above, u - oc, u + HALF)
        base = capacity + jnp.where(above, 4, 0)
        tab[at] = jnp.where(remote, base + (j >> 3), u)
        tab[at + 1] = jnp.where(remote, ((j & 7) >> 1) * TILE, CELLS - TILE)
        tab[at + 2] = jnp.where(remote & ((j & 1) == 0), 64, 0)
        for d in (1, 2):
            tab[at + 2 + d] = jnp.clip(b + up[d, HALF + pos] - HALF - pos, 0, capacity - 1)
        return jnp.where(pos == HALF - 1, 0, pos + 1)

    lax.fori_loop(0, capacity, block_src, start_run)

    for d in (1, 2):

        def link(t, counts):
            r_up, r_dn = counts
            u = up[d, HALF + t] - HALF

            def put(b, side, k):
                at = T_SRC + 8 * jnp.clip(b, 0, capacity - 1) + 2 + d
                tab[at] = face_slot(capacity, d, side) + k

            cross = (t < end_run) & (u >= end_run)

            @pl.when(cross)
            def _():
                put(oc - end_run + t, 1, r_dn)

            r_dn = r_dn + cross.astype(jnp.int32)
            cross = (t >= start_run) & (u < start_run)

            @pl.when(cross)
            def _():
                put(t - start_run, 0, r_up)

            return r_up + cross.astype(jnp.int32), r_dn

        r_up, r_dn = lax.fori_loop(0, HALF, link, (zero, zero))
        tab[T_GOT + 2 * (d - 1)] = jnp.minimum(r_up, YZ)
        tab[T_GOT + 2 * (d - 1) + 1] = jnp.minimum(r_dn, YZ)


def face_slot(capacity, d, side):
    return capacity + PACKED + ((d - 1) * 2 + side) * YZ


def unpack(capacity, tab, targets):
    for d in (1, 2):
        for side in range(2):
            ref = targets[d]

            def face(k, carry, d=d, side=side, ref=ref):
                slot = capacity + 4 * side + 1 + d
                for t in range(TILES):
                    at = pl.ds(t * TILE, TILE)
                    value = pltpu.roll(ref[slot, :, at], STRIDES[d] * (EDGE - 1 - k), 1)
                    ref[face_slot(capacity, d, side) + k, :, at] = value
                return carry

            lax.fori_loop(0, tab[T_GOT + 2 * (d - 1) + side], face, 0)


def pull(value, face, last, lane):
    mixed = jnp.where(last, face, value)
    return jnp.take_along_axis(
        mixed, jnp.broadcast_to(lane, mixed.shape), axis=1, mode="promise_in_bounds"
    )


def pull_lanes(d):
    lane = lax.broadcasted_iota(jnp.int32, (1, TILE), 1)
    stride = STRIDES[d]
    coord = lane_coord(d)
    return coord == EDGE - 1, jnp.where(coord == 0, lane + stride * (EDGE - 1), lane - stride)


def pack(oc, sends, field, outs):
    low = low_half()
    coords = [lane_coord(d) for d in range(3)]
    last = pl.ds(CELLS - TILE, TILE)

    def faces(jp, carry):
        for side in range(2):
            first = (oc - HALF if side == 0 else 0) + 2 * jp
            a = field(first, 0, last)
            b = field(first + 1, 0, last)
            for part in range(len(a)):
                lane = pl.multiple_of(part * PACK + jp * TILE, TILE)
                outs[side][:, pl.ds(lane, TILE)] = jnp.where(low, pltpu.roll(a[part], 64, 1), b[part])
        return carry

    lax.fori_loop(0, HALF // 2, faces, 0)
    for side in range(2):
        for d in (1, 2):

            def cross(k, carry, side=side, d=d):
                block = sends[S_LIST + side * 16 + (d - 1) * 8 + k]
                shift = TILE - STRIDES[d] * (EDGE - 1) + STRIDES[d] * k
                for t in range(TILES):
                    values = field(block, d, pl.ds(t * TILE, TILE))
                    for part, value in enumerate(values):
                        lane = part * PACK + XFACES + (d - 1) * CELLS + t * TILE
                        at = pl.ds(lane, TILE)
                        keep = outs[side][:, at]
                        outs[side][:, at] = jnp.where(coords[d] == k, pltpu.roll(value, shift, 1), keep)
                return carry

            lax.fori_loop(0, sends[S_COUNT + side * 2 + d - 1], cross, 0)


def faces_kernel(n, capacity, old, new, upw, q0, speeds, sends, up, dn, cs):
    old_start, _, oc, _ = position(n, old, new)
    send_table(capacity, old_start, oc, upw, sends)
    for b0 in range(0, capacity, 8):
        b1 = min(b0 + 8, capacity)
        for t in range(TILES):
            at = pl.ds(t * TILE, TILE)
            cs[b0:b1, :, at] = jnp.swapaxes(speeds[:, b0:b1, at], 0, 1)

    def field(block, d, lanes):
        return (q0[block, :, lanes] * cs[block, d : d + 1, lanes],)

    pack(oc, sends, field, (up, dn))


def spread(capacity, packets, part, targets, sems):
    copies = []
    for side, packet in enumerate(packets):
        base = part * PACK
        slot = capacity + 4 * side
        pieces = (
            (0, 0, CELLS),
            (1, CELLS, XFACES - CELLS),
            (2, XFACES, CELLS),
            (3, XFACES + CELLS, CELLS),
        )
        for i, (sub, lane, width) in enumerate(pieces):
            target = targets[max(sub - 1, 0)]
            copies.append(
                pltpu.make_async_copy(
                    packet.at[:, pl.ds(base + lane, width)],
                    target.at[slot + sub, :, pl.ds(0, width)],
                    sems.at[4 * side + i],
                )
            )
    return copies


def sources(tab, b):
    at = T_SRC + 8 * b
    sx, tx, rx, sy, sz = [tab[at + i] for i in range(5)]
    return sx, pl.ds(pl.multiple_of(tx, TILE), TILE), rx, sy, sz


def first_kernel(capacity, tab, sends, q0, cs, from_prev, from_next, q1out, up, dn, qx, cx, q1, sem, sems, osems):
    load = pltpu.make_async_copy(q0, qx.at[pl.ds(0, capacity)], sem)
    load.start()

    def leave(b):
        return pltpu.make_async_copy(q1.at[b], q1out.at[b], osems.at[b])

    copies = spread(capacity, (from_prev, from_next), 0, (qx, qx, qx), sems)
    for copy in copies:
        copy.start()
    table = pltpu.make_async_copy(cs, cx.at[pl.ds(0, capacity)], sems.at[8])
    table.start()
    copies.append(table)
    for i in range(EXTRA):
        cx[capacity + i] = jnp.ones((3, CELLS), F32)
    for copy in copies:
        copy.wait()
    load.wait()
    unpack(capacity, tab, (qx, qx, qx))
    low = low_half()
    ylast, ylane = pull_lanes(1)
    zlast, zlane = pull_lanes(2)
    oc = tab[T_OC]

    def step(b, carry):
        sx, tx, rx, sy, sz = sources(tab, b)
        before = None
        for t in range(TILES):
            at = pl.ds(t * TILE, TILE)
            c = [cx[b, d : d + 1, at] for d in range(3)]
            keep = 1.0 - c[0] - c[1] - c[2]
            cuy, cuz = cx[sy, 1:2, at], cx[sz, 2:3, at]
            if t == 0:
                cux = cx[sx, 0:1, tx]
            else:
                cm = jnp.where(low, c[0], before)
            for r0, r1 in ROWSETS:
                q = qx[b, r0:r1, at]
                if t == 0:
                    far = pltpu.roll(qx[sx, r0:r1, tx] * cux, rx, 1)
                    mixed = jnp.where(low, q * c[0], far)
                else:
                    mixed = jnp.where(low, q, qx[b, r0:r1, pl.ds((t - 1) * TILE, TILE)]) * cm
                inx = pltpu.roll(mixed, 64, 1)
                iny = pull(q * c[1], qx[sy, r0:r1, at] * cuy, ylast, ylane)
                inz = pull(q * c[2], qx[sz, r0:r1, at] * cuz, zlast, zlane)
                q1[b, r0:r1, at] = q * keep + (inx + (iny + inz))
            before = c[0]
        leave(b).start()
        return carry

    lax.fori_loop(0, oc, step, 0)

    def field(block, d, lanes):
        q = q1[block, :, lanes]
        c = cx[block, d : d + 1, lanes]
        m = q - pltpu.roll(q, STRIDES[d], 1)
        m = jnp.maximum(jnp.minimum(m, q), 0.0)
        return c * q + (0.5 * c * (1.0 - c)) * m, q

    pack(oc, sends, field, (up, dn))

    def left(b, carry):
        leave(b).wait()
        return carry

    lax.fori_loop(0, oc, left, 0)


def second_kernel(
    capacity, tab, q1, cs, from_prev, from_next, q2out, *rest
):
    chunks = HALF // CHUNK
    ups, dns = rest[:chunks], rest[chunks : 2 * chunks]
    qx, fx, fy, fz, q2, tails, sem, lsems, fsems, osems, msems = rest[2 * chunks :]
    fluxes = (fx, fy, fz)
    packets = (from_prev, from_next)
    load = pltpu.make_async_copy(q1, qx.at[pl.ds(0, capacity)], sem)
    load.start()
    copies = spread(capacity, packets, 1, (qx, qx, qx), lsems)
    copies += spread(capacity, packets, 0, fluxes, fsems)
    for copy in copies:
        copy.start()
    for copy in copies:
        copy.wait()
    load.wait()
    unpack(capacity, tab, (qx, qx, qx))
    unpack(capacity, tab, fluxes)

    def leave(b):
        return pltpu.make_async_copy(q2.at[b], q2out.at[b], osems.at[b])

    low = low_half()
    ylast, ylane = pull_lanes(1)
    zlast, zlane = pull_lanes(2)
    oc = tab[T_OC]

    def limit(b, carry):
        sx, tx, rx, sy, sz = sources(tab, b)
        for t in range(TILES):
            at = pl.ds(t * TILE, TILE)
            c = [cs[b, d : d + 1, at] for d in range(3)]
            half = [0.5 * v * (1.0 - v) for v in c]
            for r0, r1 in ROWSETS:
                q = qx[b, r0:r1, at]
                if t == 0:
                    far = pltpu.roll(qx[sx, r0:r1, tx], rx, 1)
                else:
                    far = qx[b, r0:r1, pl.ds((t - 1) * TILE, TILE)]
                before = (
                    pltpu.roll(jnp.where(low, q, far), 64, 1),
                    pull(q, qx[sy, r0:r1, at], ylast, ylane),
                    pull(q, qx[sz, r0:r1, at], zlast, zlane),
                )
                rest = q
                for d in range(3):
                    m = jnp.maximum(jnp.minimum(q - before[d], q), 0.0)
                    flux = c[d] * q + half[d] * m
                    fluxes[d][b, r0:r1, at] = flux
                    rest = rest - flux
                q2[b, r0:r1, at] = rest
        return carry

    lax.fori_loop(0, oc, limit, 0)

    def step(b, carry):
        sx, tx, rx, sy, sz = sources(tab, b)
        for t in range(TILES):
            at = pl.ds(t * TILE, TILE)
            for r0, r1 in ROWSETS:
                if t == 0:
                    far = pltpu.roll(fx[sx, r0:r1, tx], rx, 1)
                else:
                    far = fx[b, r0:r1, pl.ds((t - 1) * TILE, TILE)]
                inx = pltpu.roll(jnp.where(low, fx[b, r0:r1, at], far), 64, 1)
                iny = pull(fy[b, r0:r1, at], fy[sy, r0:r1, at], ylast, ylane)
                inz = pull(fz[b, r0:r1, at], fz[sz, r0:r1, at], zlast, zlane)
                q2[b, r0:r1, at] = q2[b, r0:r1, at] + (inx + (iny + inz))
        leave(b).start()
        return carry

    lax.fori_loop(0, oc, step, 0)
    outs = []
    for side, refs in enumerate((ups, dns)):
        first = oc - HALF if side == 0 else 0
        for c in range(chunks):
            for i in range(CHUNK):
                block = first + c * CHUNK + i
                outs.append(
                    pltpu.make_async_copy(
                        q2.at[block, pl.ds(0, MAIN)],
                        refs[c].at[pl.ds(MAIN * i, MAIN)],
                        msems.at[side, c, i],
                    )
                )
                tails[side, c, 2 * i : 2 * i + 2, :] = q2[block, MAIN:BINS, :]
            outs.append(
                pltpu.make_async_copy(
                    tails.at[side, c],
                    refs[c].at[pl.ds(MAIN * CHUNK, TAIL)],
                    msems.at[side, c, CHUNK],
                )
            )
    for copy in outs:
        copy.start()
    for copy in outs:
        copy.wait()

    def left(b, carry):
        leave(b).wait()
        return carry

    lax.fori_loop(0, oc, left, 0)


def build_pairs(q, qp, pairs):
    qp[0:BINS, :] = q
    qp[BINS:ROWS, :] = jnp.zeros((ROWS - BINS, CELLS), F32)
    pending = []

    def emit(term):
        pending.append(term)
        if len(pending) % 2 == 0:
            at = 8 * (len(pending) - 2)
            tile = jnp.concatenate(pending[-2:], axis=0)
            pairs[at : at + 16, :] = tile.astype(jnp.bfloat16)

    def lead(i):
        return jnp.broadcast_to(qp[i : i + 1, :], (8, CELLS))

    def group(g):
        return qp[8 * g : 8 * g + 8, :]

    for a in range(7):
        for r in range(8):
            by = lead(8 * a + r)
            for b in range(a + 1, 8):
                emit(by * group(b))
    for e in (BINS - 2, BINS - 1):
        by = lead(e)
        for a in range(8):
            emit(by * group(a))
    for a in range(8):
        g = group(a)
        emit(g * g)
        for k in range(1, 5):
            emit(g * pltpu.roll(g, 8 - k, 0))
    tail = group(8)
    emit(tail * tail)
    emit(lead(BINS - 1) * tail)
    while len(pending) < GROUPS:
        emit(jnp.zeros((8, CELLS), F32))


def coalesce(count, load, slot_of, w, out, qps, pairs, res, sems):
    def copy_out(slot, buf):
        return pltpu.make_async_copy(res.at[buf], out.at[slot], sems.at[buf])

    def body(it, carry):
        first = 2 * it
        items = (first, jnp.minimum(first + 1, count - 1))
        values = [load(i) for i in items]

        @pl.when(it > 0)
        def _():
            for buf in range(2):
                copy_out(0, buf).wait()

        for buf in range(2):
            build_pairs(values[buf], qps[buf], pairs[buf])
        for buf in range(2):
            gain = jnp.dot(w[...], pairs[buf][...], preferred_element_type=F32)
            res[buf] = qps[buf][0:BINS, :] + gain
        copy_out(slot_of(items[0]), 0).start()

        @pl.when(first + 1 < count)
        def _():
            copy_out(slot_of(items[1]), 1).start()

        return carry

    trips = lax.div(count + 1, 2)
    lax.fori_loop(0, trips, body, 0)

    @pl.when(trips > 0)
    def _():
        copy_out(0, 0).wait()

    @pl.when((trips > 0) & (lax.rem(count, 2) == 0))
    def _():
        copy_out(0, 1).wait()


def ranges(tab):
    oc, nc, old, new = tab[T_OC], tab[T_NC], tab[T_OS], tab[T_NS]
    lo = jnp.clip(old - new, 0, nc)
    hi = jnp.clip(old + oc - new, lo, nc)
    return lo, hi, nc, new - old


def stay_kernel(capacity, tab, q2, w, out, qpa, qpb, pa, pb, res, zero, sems, zsem):
    lo, hi, nc, shift = ranges(tab)
    zero[...] = jnp.zeros_like(zero)

    def blank(slot):
        return pltpu.make_async_copy(zero, out.at[slot], zsem)

    def start(slot, carry):
        blank(slot).start()
        return carry

    def wait(slot, carry):
        blank(slot).wait()
        return carry

    lax.fori_loop(nc, capacity, start, 0)
    coalesce(
        hi - lo,
        lambda i: q2[i + lo + shift],
        lambda i: i + lo,
        w,
        out,
        (qpa, qpb),
        (pa, pb),
        res,
        sems,
    )
    lax.fori_loop(nc, capacity, wait, 0)


def come_kernel(c, tab, from_prev, from_next, w, old_out, out, qpa, qpb, pa, pb, res, src, tails, sems, lsems):
    lo, hi, nc, _ = ranges(tab)
    loads = []
    for side, ref in enumerate((from_prev, from_next)):
        for i in range(CHUNK):
            loads.append(
                pltpu.make_async_copy(
                    ref.at[pl.ds(MAIN * i, MAIN)],
                    src.at[side * CHUNK + i, pl.ds(0, MAIN)],
                    lsems.at[side, i],
                )
            )
        loads.append(
            pltpu.make_async_copy(
                ref.at[pl.ds(MAIN * CHUNK, TAIL)], tails.at[side], lsems.at[side, CHUNK]
            )
        )
    for copy in loads:
        copy.start()
    for copy in loads:
        copy.wait()
    for side in range(2):
        for i in range(CHUNK):
            src[side * CHUNK + i, MAIN:BINS, :] = tails[side, 2 * i : 2 * i + 2, :]
    skip = jnp.clip(HALF - lo - c * CHUNK, 0, CHUNK)
    ups = CHUNK - skip
    downs = jnp.clip(nc - hi - c * CHUNK, 0, CHUNK)
    slot_up = c * CHUNK + skip - HALF + lo
    slot_dn = hi + c * CHUNK
    coalesce(
        ups + downs,
        lambda i: src[jnp.where(i < ups, i + skip, i - ups + CHUNK)],
        lambda i: jnp.where(i < ups, i + slot_up, i - ups + slot_dn),
        w,
        out,
        (qpa, qpb),
        (pa, pb),
        res,
        sems,
    )


def diagonal_picks():
    row = lax.broadcasted_iota(jnp.int32, (64, 40), 0)
    col = lax.broadcasted_iota(jnp.int32, (64, 40), 1)
    i, j, k, s = row // 8, row % 8, col // 8, col % 8
    t = (s + k) % 8
    direct = (i == s) & (j == t)
    mirror = (i == t) & (j == s) & (k > 0) & (k < 4)
    return (direct | mirror).astype(jnp.bfloat16)


def mirrored(narrow):
    cube = narrow.astype(F32)
    return (cube + jnp.swapaxes(cube, 1, 2)).astype(jnp.bfloat16)


def folded_kernel(narrow, both):
    cube = narrow
    a, b = BINS - 2, BINS - 1
    parts = [both[:, 8 * g : 8 * g + 8, 8 * g + 8 : a].reshape(BINS, -1) for g in range(7)]
    parts += [both[:, a, :a], both[:, b, :a]]
    spans = [slice(8 * g, 8 * g + 8) for g in range(8)]
    blocks = jnp.stack([narrow[:, at, at] for at in spans], axis=1).reshape(BINS * 8, 64)
    pick = lax.dot(blocks, diagonal_picks(), preferred_element_type=F32)
    parts.append(pick.reshape(BINS, 8 * 40))
    zero = jnp.zeros((BINS, 6), jnp.bfloat16)
    parts += [cube[:, a, a][:, None], cube[:, b, b][:, None], zero]
    parts += [both[:, a, b][:, None], jnp.zeros((BINS, 7), jnp.bfloat16)]
    width = sum(p.shape[1] for p in parts)
    parts.append(jnp.zeros((BINS, KDIM - width), F32))
    return jnp.concatenate([p.astype(jnp.bfloat16) for p in parts], axis=1)


def on_device(n, spectra, courant, kernel, old_count, new_count, upwind):
    capacity = spectra.shape[0]
    shape = jax.ShapeDtypeStruct
    vmem = pl.BlockSpec(memory_space=pltpu.VMEM)
    smem = pl.BlockSpec(memory_space=pltpu.SMEM)
    hbm = pl.BlockSpec(memory_space=pl.ANY)
    params = pltpu.CompilerParams(vmem_limit_bytes=VMEM_LIMIT)
    blocks = shape((capacity, BINS, CELLS), F32)
    chunk = shape((CHUNK * MAIN + TAIL, CELLS), F32)
    chunks = HALF // CHUNK
    wide = pltpu.VMEM((capacity + EXTRA, BINS, CELLS), F32)
    dma = pltpu.SemaphoreType.DMA

    def cost(flops, nbytes):
        return pl.CostEstimate(flops=flops, bytes_accessed=nbytes, transcendentals=0)

    upw = jnp.swapaxes(upwind, 0, 1)
    sends, up, dn, cs = pl.pallas_call(
        functools.partial(faces_kernel, n, capacity),
        out_shape=(
            shape((S_LIST + 32,), jnp.int32),
            shape((BINS, PACK), F32),
            shape((BINS, PACK), F32),
            shape((capacity, 3, CELLS), F32),
        ),
        in_specs=[smem, smem, smem, vmem, vmem],
        out_specs=(smem, vmem, vmem, vmem),
        compiler_params=params,
        name="faces",
    )(old_count, new_count, upw, spectra, jnp.swapaxes(courant, 0, 1))

    def along(value, step, ring):
        route = [(i, i + step) for i in range(n)]
        if ring:
            route = [(i, j % n) for i, j in route]
        return lax.ppermute(value, "blocks", [(i, j) for i, j in route if 0 <= j < n])

    from_prev, from_next = along(up, 1, True), along(dn, -1, True)
    tab = pl.pallas_call(
        functools.partial(plan_kernel, n, capacity),
        out_shape=shape((T_SRC + 8 * capacity,), jnp.int32),
        in_specs=[smem] * 4,
        out_specs=smem,
        cost_estimate=cost(1000000, 1000000),
        name="plan",
    )(sends, old_count, new_count, upw)
    cube = kernel.reshape(BINS, BINS, BINS)
    both = mirrored(cube)
    packed = shape((BINS, 2 * PACK), F32)
    q1, up, dn = pl.pallas_call(
        functools.partial(first_kernel, capacity),
        out_shape=(blocks, packed, packed),
        in_specs=[smem, smem, hbm, hbm, hbm, hbm],
        out_specs=(hbm, vmem, vmem),
        scratch_shapes=[
            wide,
            pltpu.VMEM((capacity + EXTRA, 3, CELLS), F32),
            pltpu.VMEM((capacity, BINS, CELLS), F32),
            dma,
            dma((9,)),
            dma((capacity,)),
        ],
        compiler_params=params,
        name="first",
    )(tab, sends, spectra, cs, from_prev, from_next)
    from_prev, from_next = along(up, 1, True), along(dn, -1, True)
    q1, cube, both = lax.optimization_barrier((q1, cube, both))
    q1, weights = lax.optimization_barrier((q1, folded_kernel(cube, both)))
    q2, *moved = pl.pallas_call(
        functools.partial(second_kernel, capacity),
        out_shape=[blocks] + [chunk] * (2 * chunks),
        in_specs=[smem, hbm, vmem, hbm, hbm],
        out_specs=[hbm] * (1 + 2 * chunks),
        scratch_shapes=[
            wide,
            pltpu.VMEM((capacity + PACKED, BINS, CELLS), F32),
            wide,
            wide,
            pltpu.VMEM((capacity, BINS, CELLS), F32),
            pltpu.VMEM((2, chunks, TAIL, CELLS), F32),
            dma,
            dma((8,)),
            dma((8,)),
            dma((capacity,)),
            dma((2, chunks, CHUNK + 1)),
        ],
        compiler_params=params,
        name="second",
    )(tab, q1, cs, from_prev, from_next)
    arrived = [
        (along(moved[c], 1, False), along(moved[chunks + c], -1, False)) for c in range(chunks)
    ]
    buffers = [
        pltpu.VMEM((ROWS, CELLS), F32),
        pltpu.VMEM((ROWS, CELLS), F32),
        pltpu.VMEM((KDIM, CELLS), jnp.bfloat16),
        pltpu.VMEM((KDIM, CELLS), jnp.bfloat16),
        pltpu.VMEM((2, BINS, CELLS), F32),
    ]
    work = 2 * BINS * KDIM * CELLS
    updated = pl.pallas_call(
        functools.partial(stay_kernel, capacity),
        out_shape=blocks,
        in_specs=[smem, vmem, vmem],
        out_specs=hbm,
        scratch_shapes=buffers + [pltpu.VMEM((BINS, CELLS), F32), dma((2,)), dma],
        compiler_params=params,
        cost_estimate=cost(24 * work, 12 * 1024 * 1024),
        name="stay",
    )(tab, q2, weights)
    for c in range(chunks):
        updated = pl.pallas_call(
            functools.partial(come_kernel, c),
            out_shape=blocks,
            in_specs=[smem, hbm, hbm, vmem, hbm],
            out_specs=hbm,
            input_output_aliases={4: 0},
            scratch_shapes=buffers
            + [
                pltpu.VMEM((2 * CHUNK, BINS, CELLS), F32),
                pltpu.VMEM((2, TAIL, CELLS), F32),
                dma((2,)),
                dma((2, CHUNK + 1)),
            ],
            compiler_params=params,
            cost_estimate=cost(2 * CHUNK * work, 4 * 1024 * 1024),
            name=f"come{c}",
        )(tab, *arrived[c], weights, updated)
    return updated


def solution(mesh):
    in_specs = (P("blocks", None, None), P("blocks", None, None), P(), P(), P(), P())
    out_specs = P("blocks", None, None)
    return jax.shard_map(
        functools.partial(on_device, mesh.shape["blocks"]),
        mesh=mesh,
        in_specs=in_specs,
        out_specs=out_specs,
        check_vma=False,
    )
```
